256 devices in a mesh: dp: 16 (over y, x_lo, core), feat: 16 (over x_hi, z).
Axes of the slice: x: 4 (x_hi: 2, x_lo: 2; x = x_hi * 2 + x_lo), y: 4, z: 8, core: 2. Of those that a mesh axis runs over, the one named last changes fastest.
Arguments:
- tokens: bfloat16 [8192, 16384], P('dp', 'feat'), may hold values from -6 to 6
- weight: bfloat16 [32, 6, 512, 512], P('feat'), may hold values from -0.15625 to 0.15625
- cotangent: bfloat16 [8192, 16384], P('dp', 'feat'), may hold values from -6 to 6
Outputs:
- output: bfloat16 [8192, 16384], P('dp', 'feat')
- input_grad: bfloat16 [8192, 16384], P('dp', 'feat')
- weight_grad: float32 [32, 6, 512, 512], P('feat', None, 'dp')
The draws below stay inside these ranges and needn't reach their ends.
All inputs are finite; a program needn't handle non-finite values.
Results may differ from the reference program's by a relative error of at most 0.0057.
Values may be sent and summed in bfloat16 or wider, within the bound.
A program may use at most 128 MiB of HBM per device.

```python
from functools import partial
import jax
import jax.numpy as jnp
import numpy as np

BLK = 512
NB = 32
PARTNERS = 6
D = 16384
TOKENS = 8192


def levels(key, extent, split, least, largest):
    loudness, own = 1.0, jax.random.fold_in(key, 6)
    for dim, parts in split:
        steps = jnp.exp(jax.random.uniform(jax.random.fold_in(own, dim), (parts,), jnp.float32, least / len(split), largest / len(split)))
        loudness = loudness * jnp.repeat(steps, extent[dim] // parts).reshape([-1 if axis == dim else 1 for axis in range(len(extent))])
    return loudness


def centred(stream_key, extent, scale, limit, split=(), dtype=jnp.bfloat16):
    level = levels(stream_key, extent, split, -0.22, 0.18) if split else 1.0
    array = jax.random.normal(stream_key, extent, jnp.float32) * scale * level
    return jnp.minimum(jnp.maximum(array, -limit), limit).astype(dtype)


def setup_inputs(seed: int = 0) -> dict:
    splits = jax.random.split(jax.random.key(seed), 4)
    tokens = centred(splits[0], (TOKENS, D), 1.0, 6.0, ((0, 16), (1, 16)))
    weight = centred(splits[1], (NB, PARTNERS, BLK, BLK), (PARTNERS * BLK // 2) ** -0.5, 0.15625, ((0, 16),))
    cotangent = centred(splits[2], (TOKENS, D), 1.0, 6.0, ((0, 16), (1, 16)))
    return {"tokens": tokens, "weight": weight, "cotangent": cotangent}


gelu_tanh = partial(jax.nn.gelu, approximate=True)

def partner_order(which):
    if which == 0:
        return np.arange(NB)
    return np.arange(NB) ^ 1 << which - 1

def mix_layer(blocks, weight):
    total = jnp.zeros((blocks.shape[0], NB, BLK), jnp.float32)
    for which in range(PARTNERS):
        moved = blocks[:, partner_order(which), :].astype(jnp.float32)
        total = total + jnp.einsum('tnb,nbc->tnc', moved, weight[:, which].astype(jnp.float32))
    return total

def weight_grads(blocks, delta):
    stacked = []
    for which in range(PARTNERS):
        moved = blocks[:, partner_order(which), :].astype(jnp.float32)
        stacked.append(jnp.einsum('tnb,tnc->nbc', moved, delta.astype(jnp.float32)))
    return jnp.stack(stacked, axis=1)

def back_sum(delta, weight):
    total = jnp.zeros(delta.shape, jnp.float32)
    for which in range(PARTNERS):
        term = jnp.einsum('tnc,nbc->tnb', delta.astype(jnp.float32), weight[:, which].astype(jnp.float32))
        term = term.astype(jnp.bfloat16)
        total = total + term[:, partner_order(which), :].astype(jnp.float32)
    return total

def reference(tokens, weight, cotangent):
    inputs = tokens.reshape(TOKENS, NB, BLK)
    z_value = mix_layer(inputs, weight)
    output = gelu_tanh(z_value).astype(jnp.bfloat16)
    unused, pull_back = jax.vjp(gelu_tanh, z_value)
    delta = pull_back(cotangent.reshape(TOKENS, NB, BLK).astype(jnp.float32))[0].astype(jnp.bfloat16)
    weight_grad = weight_grads(inputs, delta)
    input_grad = back_sum(delta, weight).astype(jnp.bfloat16)
    return (output.reshape(TOKENS, D), input_grad.reshape(TOKENS, D), weight_grad)
```

```python
import functools

import jax
import jax.numpy as jnp
from jax import lax
from jax.experimental import pallas as pl
from jax.experimental.pallas import tpu as pltpu
from jax.sharding import PartitionSpec as P

F32 = jnp.float32
BF16 = jnp.bfloat16
MESH = pl.DeviceIdType.MESH
BLK = 512
PARTNERS = 6
CHUNKS = 8
REMOTE = 4
CHIPS = 8
SLOPE = 0.7978845608028654
CUBE = 0.044715


def flip(value, bit):
    return value + bit - 2 * bit * ((value // bit) % 2)


def nn(a, b):
    return lax.dot_general(a, b, (((1,), (0,)), ((), ())), preferred_element_type=F32)


def nt(a, b):
    return lax.dot_general(a, b, (((1,), (1,)), ((), ())), preferred_element_type=F32)


def tn(a, b):
    return lax.dot_general(a, b, (((0,), (0,)), ((), ())), preferred_element_type=F32)


def kernel(
    tok_hbm, w_hbm, cot_hbm, out_hbm, ig_hbm, wg_hbm,
    tok, w, cot, trecv, delta, outv, acc, tsend, termrecv, mine, other, crecv, total, rsrecv, wgv,
    load_sem, store_sem, tok_ssem, tok_rsem, term_ssem, term_rsem, c_ssem, c_rsem, rs_ssem, rs_rsem,
):
    rows = tok.shape[0] // CHUNKS
    d = lax.axis_index("dp")
    f = lax.axis_index("feat")
    core = d % 2
    chip = d // 2
    y = chip // 2
    x_lo = chip % 2

    partners = [(d, flip(f, 1 << b)) for b in range(REMOTE)]
    core_mate = (flip(d, 1), f)

    def chip_of(j):
        dy, dx = j // 2, j % 2
        return ((y + dy) % 4) * 2 + (x_lo + dx) % 2

    def mate(j):
        return (chip_of(j) * 2 + core, f)

    everyone = partners + [core_mate]
    barrier = pltpu.get_barrier_semaphore()
    for who in everyone:
        pl.semaphore_signal(barrier, inc=1, device_id=who, device_id_type=MESH)
    for j in range(1, CHIPS):
        pl.semaphore_signal(barrier, inc=1, device_id=mate(j), device_id_type=MESH)

    load_tok = pltpu.make_async_copy(tok_hbm, tok, load_sem.at[0])
    load_w = pltpu.make_async_copy(w_hbm, w, load_sem.at[1])
    load_cot = pltpu.make_async_copy(cot_hbm, cot, load_sem.at[2])
    load_tok.start()
    load_w.start()
    load_cot.start()
    pl.semaphore_wait(barrier, len(everyone) + CHIPS - 1)
    load_tok.wait()

    def span(c):
        return pl.ds(pl.multiple_of(c * rows, rows), rows)

    def tok_copy(b, c):
        return pltpu.make_async_remote_copy(
            src_ref=tok.at[span(c)], dst_ref=trecv.at[b, span(c)],
            send_sem=tok_ssem.at[b, c], recv_sem=tok_rsem.at[b, c],
            device_id=partners[b], device_id_type=MESH,
        )

    def term_copy(b, c):
        return pltpu.make_async_remote_copy(
            src_ref=tsend.at[b, span(c)], dst_ref=termrecv.at[b, span(c)],
            send_sem=term_ssem.at[b, c], recv_sem=term_rsem.at[b, c],
            device_id=partners[b], device_id_type=MESH,
        )

    @pl.loop(0, CHUNKS)
    def _(c):
        for b in (2, 1, 0, 3):
            tok_copy(b, c).start()

    load_w.wait()
    load_cot.wait()

    def half(n):
        return pl.ds(n * BLK, BLK)

    @pl.loop(0, CHUNKS)
    def _(c):
        here = span(c)
        for b in range(REMOTE):
            tok_copy(b, c).wait_recv()
        for n in range(2):
            z = nn(tok[here, half(n)], w[n, 0]) + nn(tok[here, half(1 - n)], w[n, 1])
            for b in range(REMOTE):
                z = z + nn(trecv[b, here, half(n)], w[n, b + 2])
            square = z * z
            t = jnp.tanh(SLOPE * (z + CUBE * (square * z)))
            outv[here, half(n)] = (0.5 * z * (1.0 + t)).astype(BF16)
            slope = 0.5 * (1.0 + t) + 0.5 * z * (1.0 - t * t) * (SLOPE * (1.0 + 3.0 * CUBE * square))
            delta[here, half(n)] = (cot[here, half(n)].astype(F32) * slope).astype(BF16)
        for b in (2, 1, 0, 3):
            for n in range(2):
                tsend[b, here, half(n)] = nt(delta[here, half(n)], w[n, b + 2]).astype(BF16)
            term_copy(b, c).start()
        for n in range(2):
            own = nt(delta[here, half(n)], w[n, 0]).astype(BF16).astype(F32)
            side = nt(delta[here, half(1 - n)], w[1 - n, 1]).astype(BF16).astype(F32)
            acc[here, half(n)] = own + side

    store_out = pltpu.make_async_copy(outv, out_hbm, store_sem.at[0])
    store_out.start()

    def core_copy(k):
        return pltpu.make_async_remote_copy(
            src_ref=other.at[k], dst_ref=crecv.at[k],
            send_sem=c_ssem.at[k], recv_sem=c_rsem.at[k],
            device_id=core_mate, device_id_type=MESH,
        )

    def rs_copy(k, j):
        return pltpu.make_async_remote_copy(
            src_ref=total.at[k, chip_of(j)], dst_ref=rsrecv.at[j - 1, k],
            send_sem=rs_ssem.at[j - 1, k], recv_sem=rs_rsem.at[j - 1, k],
            device_id=mate(j), device_id_type=MESH,
        )

    for k in range(PARTNERS):
        for n in range(2):
            if k == 0:
                left = tok[:, half(n)]
            elif k == 1:
                left = tok[:, half(1 - n)]
            else:
                left = trecv[k - 2, :, half(n)]
            grad = tn(left, delta[:, half(n)])
            grad = grad.reshape(CHIPS, 2, BLK // 16, BLK)
            even, odd = grad[:, 0], grad[:, 1]
            mine[k, :, n] = jnp.where(core == 0, even, odd)
            other[k, :, n] = jnp.where(core == 0, odd, even).astype(BF16)
        core_copy(k).start()

    @pl.loop(0, PARTNERS)
    def _(k):
        core_copy(k).wait_recv()
        for q in range(CHIPS):
            both = mine[k, q] + crecv[k, q].astype(F32)
            mine[k, q] = both
            total[k, q] = both.astype(BF16)
        for j in range(1, CHIPS):
            rs_copy(k, j).start()

    @pl.loop(0, CHUNKS)
    def _(c):
        here = span(c)
        for b in range(REMOTE):
            term_copy(b, c).wait_recv()
        result = acc[here, :]
        for b in range(REMOTE):
            result = result + termrecv[b, here].astype(F32)
        cot[here, :] = result.astype(BF16)

    store_ig = pltpu.make_async_copy(cot, ig_hbm, store_sem.at[1])
    store_ig.start()

    @pl.loop(0, PARTNERS)
    def _(k):
        for j in range(1, CHIPS):
            rs_copy(k, j).wait_recv()
        summed = mine[k, chip]
        for j in range(1, CHIPS):
            summed = summed + rsrecv[j - 1, k].astype(F32)
        for n in range(2):
            wgv[n, k] = summed[n]

    store_wg = pltpu.make_async_copy(wgv, wg_hbm, store_sem.at[2])
    store_wg.start()

    @pl.loop(0, CHUNKS)
    def _(c):
        for b in range(REMOTE):
            tok_copy(b, c).wait_send()
            term_copy(b, c).wait_send()

    @pl.loop(0, PARTNERS)
    def _(k):
        core_copy(k).wait_send()
        for j in range(1, CHIPS):
            rs_copy(k, j).wait_send()

    store_out.wait()
    store_ig.wait()
    store_wg.wait()


def local(tokens, weight, cotangent):
    r, width = tokens.shape
    strip = BLK // 16
    dma = pltpu.SemaphoreType.DMA
    return pl.pallas_call(
        kernel,
        out_shape=(
            jax.ShapeDtypeStruct((r, width), BF16),
            jax.ShapeDtypeStruct((r, width), BF16),
            jax.ShapeDtypeStruct((2, PARTNERS, strip, BLK), F32),
        ),
        in_specs=[pl.BlockSpec(memory_space=pl.ANY)] * 3,
        out_specs=[pl.BlockSpec(memory_space=pl.ANY)] * 3,
        scratch_shapes=[
            pltpu.VMEM((r, width), BF16),
            pltpu.VMEM(weight.shape, BF16),
            pltpu.VMEM((r, width), BF16),
            pltpu.VMEM((REMOTE, r, width), BF16),
            pltpu.VMEM((r, width), BF16),
            pltpu.VMEM((r, width), BF16),
            pltpu.VMEM((r, width), F32),
            pltpu.VMEM((REMOTE, r, width), BF16),
            pltpu.VMEM((REMOTE, r, width), BF16),
            pltpu.VMEM((PARTNERS, CHIPS, 2, strip, BLK), F32),
            pltpu.VMEM((PARTNERS, CHIPS, 2, strip, BLK), BF16),
            pltpu.VMEM((PARTNERS, CHIPS, 2, strip, BLK), BF16),
            pltpu.VMEM((PARTNERS, CHIPS, 2, strip, BLK), BF16),
            pltpu.VMEM((CHIPS - 1, PARTNERS, 2, strip, BLK), BF16),
            pltpu.VMEM((2, PARTNERS, strip, BLK), F32),
            dma((3,)),
            dma((3,)),
            dma((REMOTE, CHUNKS)),
            dma((REMOTE, CHUNKS)),
            dma((REMOTE, CHUNKS)),
            dma((REMOTE, CHUNKS)),
            dma((PARTNERS,)),
            dma((PARTNERS,)),
            dma((CHIPS - 1, PARTNERS)),
            dma((CHIPS - 1, PARTNERS)),
        ],
        compiler_params=pltpu.CompilerParams(
            collective_id=0, has_side_effects=True, vmem_limit_bytes=64_000_000
        ),
    )(tokens, weight, cotangent)


def solution(mesh):
    return jax.shard_map(
        local,
        mesh=mesh,
        in_specs=(P("dp", "feat"), P("feat", None, None, None), P("dp", "feat")),
        out_specs=(P("dp", "feat"), P("dp", "feat"), P("feat", None, "dp", None)),
        check_vma=False,
    )
```

```python
import functools

import jax
import jax.numpy as jnp
from jax import lax
from jax.experimental import pallas as pl
from jax.experimental.pallas import tpu as pltpu
from jax.sharding import PartitionSpec as P

F32 = jnp.float32
BF16 = jnp.bfloat16
MESH = pl.DeviceIdType.MESH
BLK = 512
PARTNERS = 6
CHUNKS = 8
LAG = 4
FLOWS = 6
CHIPS = 8
SLOPE = 0.7978845608028654
CUBE = 0.044715


def flip(value, bit):
    return value + bit - 2 * bit * ((value // bit) % 2)


def nn(a, b):
    return lax.dot_general(a, b, (((1,), (0,)), ((), ())), preferred_element_type=F32)


def nt(a, b):
    return lax.dot_general(a, b, (((1,), (1,)), ((), ())), preferred_element_type=F32)


def tn(a, b):
    return lax.dot_general(a, b, (((0,), (0,)), ((), ())), preferred_element_type=F32)


def kernel(
    tok_hbm, w_hbm, cot_hbm, out_hbm, ig_hbm, wg_hbm,
    tok, w, cot, recv, delta, outv, acc, pool, mine, other, crecv, total, rsrecv, wgv,
    load_sem, store_sem, tok_ssem, tok_rsem, term_ssem, term_rsem, c_ssem, c_rsem, rs_ssem, rs_rsem,
):
    rows = tok.shape[0] // CHUNKS
    d = lax.axis_index("dp")
    f = lax.axis_index("feat")
    core = d % 2
    chip = d // 2
    y = chip // 2
    x_lo = chip % 2
    z = f % 8
    inner = (z + z // 2) % 2
    sgn = 1 - 2 * ((z // 2) % 2)

    def along(step):
        return (d, (f // 8) * 8 + (z + step + 8) % 8)

    ahead = along(sgn)
    behind = along(-sgn)
    across = (d, flip(f, 8))
    core_mate = (flip(d, 1), f)

    def chip_of(j):
        dy, dx = j // 2, j % 2
        return ((y + dy) % 4) * 2 + (x_lo + dx) % 2

    def mate(j):
        return (chip_of(j) * 2 + core, f)

    everyone = [ahead, behind, across, core_mate]
    barrier = pltpu.get_barrier_semaphore()
    for who in everyone:
        pl.semaphore_signal(barrier, inc=1, device_id=who, device_id_type=MESH)
    for j in range(1, CHIPS):
        pl.semaphore_signal(barrier, inc=1, device_id=mate(j), device_id_type=MESH)

    load_tok = pltpu.make_async_copy(tok_hbm, tok, load_sem.at[0])
    load_w = pltpu.make_async_copy(w_hbm, w, load_sem.at[1])
    load_cot = pltpu.make_async_copy(cot_hbm, cot, load_sem.at[2])
    load_tok.start()
    load_w.start()
    load_cot.start()
    pl.semaphore_wait(barrier, len(everyone) + CHIPS - 1)
    load_tok.wait()

    def span(c):
        return pl.ds(pl.multiple_of(c * rows, rows), rows)

    def half(n):
        return pl.ds(n * BLK, BLK)

    def tok_copy(flow, c):
        source, slot, to = (
            (tok.at[span(c)], 2 * inner, ahead),
            (recv.at[0, span(c)], 2 * inner + 1, ahead),
            (recv.at[2, span(c)], 2 * inner, behind),
            (recv.at[3, span(c)], 2 * inner + 1, behind),
            (tok.at[span(c)], 4, behind),
            (tok.at[span(c)], 5, across),
        )[flow]
        return pltpu.make_async_remote_copy(
            src_ref=source, dst_ref=recv.at[slot, span(c)],
            send_sem=tok_ssem.at[flow, c], recv_sem=tok_rsem.at[slot, c],
            device_id=to, device_id_type=MESH,
        )

    def tok_wait(slot, c):
        pltpu.make_async_remote_copy(
            src_ref=recv.at[slot, span(c)], dst_ref=recv.at[slot, span(c)],
            send_sem=tok_ssem.at[0, c], recv_sem=tok_rsem.at[slot, c],
            device_id=ahead, device_id_type=MESH,
        ).wait_recv()

    def own(c):
        @pl.when(c < CHUNKS)
        def _():
            tok_copy(0, c).start()
            tok_copy(5, c).start()

            @pl.when(inner == 1)
            def _():
                tok_copy(4, c).start()

    def relay(slot, flow, c):
        @pl.when((c >= 0) & (c < CHUNKS))
        def _():
            tok_wait(slot, c)
            tok_copy(flow, c).start()

    low = 4 + 2 * (1 - inner)

    def term_copy(flow, c):
        source, slot, to = (
            (5 * (1 - inner), low, behind),
            (2, low + 1, behind),
            (1 + 5 * inner, low, ahead),
            (1 + 6 * (1 - inner), low + 1, ahead),
            (0, 8, ahead),
            (3, 9, across),
        )[flow]
        return pltpu.make_async_remote_copy(
            src_ref=pool.at[source, span(c)], dst_ref=pool.at[slot, span(c)],
            send_sem=term_ssem.at[flow, c], recv_sem=term_rsem.at[slot - 4, c],
            device_id=to, device_id_type=MESH,
        )

    def term_wait(slot, c):
        pltpu.make_async_remote_copy(
            src_ref=pool.at[slot, span(c)], dst_ref=pool.at[slot, span(c)],
            send_sem=term_ssem.at[0, c], recv_sem=term_rsem.at[slot - 4, c],
            device_id=ahead, device_id_type=MESH,
        ).wait_recv()

    def add_term(into, slot, c):
        here = span(c)
        pool[into, here] = (pool[into, here].astype(F32) + pool[slot, here].astype(F32)).astype(BF16)

    def back_relays(p):
        c0 = p - 1 - 2 * inner

        @pl.when((c0 >= 0) & (c0 < CHUNKS))
        def _():
            term_wait(5, c0)

            @pl.when(inner == 1)
            def _():
                add_term(0, 5, c0)

            term_copy(0, c0).start()

        c2 = p - 2 - inner

        @pl.when((c2 >= 0) & (c2 < CHUNKS))
        def _():
            term_wait(6, c2)

            @pl.when(inner == 0)
            def _():
                add_term(1, 6, c2)

            term_copy(2, c2).start()

        c3 = p - 1 - inner

        @pl.when((c3 >= 0) & (c3 < CHUNKS))
        def _():
            term_wait(7, c3)

            @pl.when(inner == 1)
            def _():
                add_term(1, 7, c3)

            term_copy(3, c3).start()

    def compute(c):
        here = span(c)
        tok_wait(1, c)
        tok_wait(5, c)

        @pl.when(inner == 0)
        def _():
            tok_wait(4, c)

        first = 4 * (1 - inner)
        second = 2 + inner
        for n in range(2):
            v = nn(tok[here, half(n)], w[n, 0]) + nn(tok[here, half(1 - n)], w[n, 1])
            v = v + nn(recv[first, here, half(n)], w[n, 2]) + nn(recv[second, here, half(n)], w[n, 3])
            v = v + nn(recv[1, here, half(n)], w[n, 4]) + nn(recv[5, here, half(n)], w[n, 5])
            square = v * v
            t = jnp.tanh(SLOPE * (v + CUBE * (square * v)))
            outv[here, half(n)] = (0.5 * v * (1.0 + t)).astype(BF16)
            slope = 0.5 * (1.0 + t) + 0.5 * v * (1.0 - t * t) * (SLOPE * (1.0 + 3.0 * CUBE * square))
            delta[here, half(n)] = (cot[here, half(n)].astype(F32) * slope).astype(BF16)
        for b in (2, 0, 1, 3):
            for n in range(2):
                pool[b, here, half(n)] = nt(delta[here, half(n)], w[n, b + 2]).astype(BF16)
            if b == 2:
                term_copy(1, c).start()
            if b == 0:
                @pl.when(inner == 0)
                def _():
                    term_copy(4, c).start()
            if b == 3:
                term_copy(5, c).start()
        for n in range(2):
            mid = nt(delta[here, half(n)], w[n, 0]).astype(BF16).astype(F32)
            side = nt(delta[here, half(1 - n)], w[1 - n, 1]).astype(BF16).astype(F32)
            acc[here, half(n)] = mid + side

    own(0)

    @pl.loop(0, CHUNKS + LAG)
    def _(i):
        own(i + 1)
        relay(0, 1, i - 3 + 2 * inner)
        relay(2, 2, i - 2 + inner)
        relay(3, 3, i - 3 + inner)

        @pl.when(i == LAG)
        def _():
            load_w.wait()
            load_cot.wait()

        @pl.when(i >= LAG)
        def _():
            compute(i - LAG)
            back_relays(i - LAG)

    store_out = pltpu.make_async_copy(outv, out_hbm, store_sem.at[0])
    store_out.start()

    def core_copy(k):
        return pltpu.make_async_remote_copy(
            src_ref=other.at[k], dst_ref=crecv.at[k],
            send_sem=c_ssem.at[k], recv_sem=c_rsem.at[k],
            device_id=core_mate, device_id_type=MESH,
        )

    def rs_copy(k, j):
        return pltpu.make_async_remote_copy(
            src_ref=total.at[k, chip_of(j)], dst_ref=rsrecv.at[j - 1, k],
            send_sem=rs_ssem.at[j - 1, k], recv_sem=rs_rsem.at[j - 1, k],
            device_id=mate(j), device_id_type=MESH,
        )

    first = 4 * (1 - inner)
    second = 2 + inner
    for k in range(PARTNERS):
        for n in range(2):
            if k == 0:
                left = tok[:, half(n)]
            elif k == 1:
                left = tok[:, half(1 - n)]
            else:
                left = recv[(first, second, 1, 5)[k - 2], :, half(n)]
            grad = tn(left, delta[:, half(n)])
            grad = grad.reshape(CHIPS, 2, BLK // 16, BLK)
            even, odd = grad[:, 0], grad[:, 1]
            mine[k, :, n] = jnp.where(core == 0, even, odd)
            other[k, :, n] = jnp.where(core == 0, odd, even).astype(BF16)
        core_copy(k).start()
        if k % 2 == 1:
            back_relays(CHUNKS + k // 2)

    @pl.loop(0, PARTNERS)
    def _(k):
        core_copy(k).wait_recv()
        for q in range(CHIPS):
            both = mine[k, q] + crecv[k, q].astype(F32)
            mine[k, q] = both
            total[k, q] = both.astype(BF16)
        for j in range(1, CHIPS):
            rs_copy(k, j).start()

    @pl.loop(0, CHUNKS)
    def _(c):
        here = span(c)
        term_wait(4, c)
        term_wait(9, c)

        @pl.when(inner == 1)
        def _():
            term_wait(8, c)
            acc[here, :] += pool[8, here].astype(F32)

        result = acc[here, :] + pool[4, here].astype(F32) + pool[9, here].astype(F32)
        cot[here, :] = result.astype(BF16)

    store_ig = pltpu.make_async_copy(cot, ig_hbm, store_sem.at[1])
    store_ig.start()

    @pl.loop(0, PARTNERS)
    def _(k):
        for j in range(1, CHIPS):
            rs_copy(k, j).wait_recv()
        summed = mine[k, chip]
        for j in range(1, CHIPS):
            summed = summed + rsrecv[j - 1, k].astype(F32)
        for n in range(2):
            wgv[n, k] = summed[n]

    store_wg = pltpu.make_async_copy(wgv, wg_hbm, store_sem.at[2])
    store_wg.start()

    @pl.loop(0, CHUNKS)
    def _(c):
        for flow in (0, 1, 2, 3, 5):
            tok_copy(flow, c).wait_send()
            term_copy(flow, c).wait_send()

        @pl.when(inner == 1)
        def _():
            tok_copy(4, c).wait_send()

        @pl.when(inner == 0)
        def _():
            term_copy(4, c).wait_send()

    @pl.loop(0, PARTNERS)
    def _(k):
        core_copy(k).wait_send()
        for j in range(1, CHIPS):
            rs_copy(k, j).wait_send()

    store_out.wait()
    store_ig.wait()
    store_wg.wait()


def local(tokens, weight, cotangent):
    r, width = tokens.shape
    strip = BLK // 16
    dma = pltpu.SemaphoreType.DMA
    return pl.pallas_call(
        kernel,
        out_shape=(
            jax.ShapeDtypeStruct((r, width), BF16),
            jax.ShapeDtypeStruct((r, width), BF16),
            jax.ShapeDtypeStruct((2, PARTNERS, strip, BLK), F32),
        ),
        in_specs=[pl.BlockSpec(memory_space=pl.ANY)] * 3,
        out_specs=[pl.BlockSpec(memory_space=pl.ANY)] * 3,
        scratch_shapes=[
            pltpu.VMEM((r, width), BF16),
            pltpu.VMEM(weight.shape, BF16),
            pltpu.VMEM((r, width), BF16),
            pltpu.VMEM((FLOWS, r, width), BF16),
            pltpu.VMEM((r, width), BF16),
            pltpu.VMEM((r, width), BF16),
            pltpu.VMEM((r, width), F32),
            pltpu.VMEM((4 + FLOWS, r, width), BF16),
            pltpu.VMEM((PARTNERS, CHIPS, 2, strip, BLK), F32),
            pltpu.VMEM((PARTNERS, CHIPS, 2, strip, BLK), BF16),
            pltpu.VMEM((PARTNERS, CHIPS, 2, strip, BLK), BF16),
            pltpu.VMEM((PARTNERS, CHIPS, 2, strip, BLK), BF16),
            pltpu.VMEM((CHIPS - 1, PARTNERS, 2, strip, BLK), BF16),
            pltpu.VMEM((2, PARTNERS, strip, BLK), F32),
            dma((3,)),
            dma((3,)),
            dma((FLOWS, CHUNKS)),
            dma((FLOWS, CHUNKS)),
            dma((FLOWS, CHUNKS)),
            dma((FLOWS, CHUNKS)),
            dma((PARTNERS,)),
            dma((PARTNERS,)),
            dma((CHIPS - 1, PARTNERS)),
            dma((CHIPS - 1, PARTNERS)),
        ],
        compiler_params=pltpu.CompilerParams(
            collective_id=0, has_side_effects=True, vmem_limit_bytes=64_000_000
        ),
    )(tokens, weight, cotangent)


def solution(mesh):
    return jax.shard_map(
        local,
        mesh=mesh,
        in_specs=(P("dp", "feat"), P("feat", None, None, None), P("dp", "feat")),
        out_specs=(P("dp", "feat"), P("dp", "feat"), P("feat", None, "dp", None)),
        check_vma=False,
    )
```

```python
import functools

import jax
import jax.numpy as jnp
from jax import lax
from jax.experimental import pallas as pl
from jax.experimental.pallas import tpu as pltpu
from jax.sharding import PartitionSpec as P

F32 = jnp.float32
BF16 = jnp.bfloat16
MESH = pl.DeviceIdType.MESH
BLK = 512
PARTNERS = 6
CHUNKS = 8
LAG = 4
BACK = 3
FLOWS = 6
CHIPS = 8
SLOPE = 0.7978845608028654
CUBE = 0.044715


def flip(value, bit):
    return value + bit - 2 * bit * ((value // bit) % 2)


def nn(a, b):
    return lax.dot_general(a, b, (((1,), (0,)), ((), ())), preferred_element_type=F32)


def nt(a, b):
    return lax.dot_general(a, b, (((1,), (1,)), ((), ())), preferred_element_type=F32)


def tn(a, b):
    return lax.dot_general(a, b, (((0,), (0,)), ((), ())), preferred_element_type=F32)


def kernel(
    tok_hbm, w_hbm, cot_hbm, out_hbm, ig_hbm, wg_hbm,
    tok, w, cot, recv, delta, outv, acc, pool, mine, other, crecv, total, rsrecv, wgv,
    load_sem, store_sem, tok_ssem, tok_rsem, term_ssem, term_rsem, c_ssem, c_rsem, rs_ssem, rs_rsem,
):
    rows = tok.shape[0] // CHUNKS
    d = lax.axis_index("dp")
    f = lax.axis_index("feat")
    core = d % 2
    chip = d // 2
    y = chip // 2
    x_lo = chip % 2
    z = f % 8
    inner = (z + z // 2) % 2
    sgn = 1 - 2 * ((z // 2) % 2)

    def along(step):
        return (d, (f // 8) * 8 + (z + step + 8) % 8)

    ahead = along(sgn)
    behind = along(-sgn)
    across = (d, flip(f, 8))
    core_mate = (flip(d, 1), f)

    def chip_of(j):
        dy, dx = j // 2, j % 2
        return ((y + dy) % 4) * 2 + (x_lo + dx) % 2

    def mate(j):
        return (chip_of(j) * 2 + core, f)

    everyone = [ahead, behind, across, core_mate]
    barrier = pltpu.get_barrier_semaphore()
    for who in everyone:
        pl.semaphore_signal(barrier, inc=1, device_id=who, device_id_type=MESH)
    for j in range(1, CHIPS):
        pl.semaphore_signal(barrier, inc=1, device_id=mate(j), device_id_type=MESH)

    load_tok = pltpu.make_async_copy(tok_hbm, tok, load_sem.at[0])
    load_w = pltpu.make_async_copy(w_hbm, w, load_sem.at[1])
    load_cot = pltpu.make_async_copy(cot_hbm, cot, load_sem.at[2])
    load_tok.start()
    load_w.start()
    load_cot.start()
    pl.semaphore_wait(barrier, len(everyone) + CHIPS - 1)
    load_tok.wait()

    def span(c):
        return pl.ds(pl.multiple_of(c * rows, rows), rows)

    def half(n):
        return pl.ds(n * BLK, BLK)

    def tok_copy(flow, c):
        source, slot, to = (
            (tok.at[span(c)], 2 * inner, ahead),
            (recv.at[0, span(c)], 2 * inner + 1, ahead),
            (recv.at[2, span(c)], 2 * inner, behind),
            (recv.at[3, span(c)], 2 * inner + 1, behind),
            (tok.at[span(c)], 4, behind),
            (tok.at[span(c)], 5, across),
        )[flow]
        return pltpu.make_async_remote_copy(
            src_ref=source, dst_ref=recv.at[slot, span(c)],
            send_sem=tok_ssem.at[flow, c], recv_sem=tok_rsem.at[slot, c],
            device_id=to, device_id_type=MESH,
        )

    def tok_wait(slot, c):
        pltpu.make_async_remote_copy(
            src_ref=recv.at[slot, span(c)], dst_ref=recv.at[slot, span(c)],
            send_sem=tok_ssem.at[0, c], recv_sem=tok_rsem.at[slot, c],
            device_id=ahead, device_id_type=MESH,
        ).wait_recv()

    def own(c):
        @pl.when(c < CHUNKS)
        def _():
            tok_copy(0, c).start()
            tok_copy(5, c).start()

            @pl.when(inner == 1)
            def _():
                tok_copy(4, c).start()

    def relay(slot, flow, c):
        @pl.when((c >= 0) & (c < CHUNKS))
        def _():
            tok_wait(slot, c)
            tok_copy(flow, c).start()

    low = 4 + 2 * (1 - inner)

    def term_copy(flow, c):
        source, slot, to = (
            (5 * (1 - inner), low, behind),
            (2, low + 1, behind),
            (1 + 5 * inner, low, ahead),
            (1 + 6 * (1 - inner), low + 1, ahead),
            (0, 8, ahead),
            (3, 9, across),
        )[flow]
        return pltpu.make_async_remote_copy(
            src_ref=pool.at[source, span(c)], dst_ref=pool.at[slot, span(c)],
            send_sem=term_ssem.at[flow, c], recv_sem=term_rsem.at[slot - 4, c],
            device_id=to, device_id_type=MESH,
        )

    def term_wait(slot, c):
        pltpu.make_async_remote_copy(
            src_ref=pool.at[slot, span(c)], dst_ref=pool.at[slot, span(c)],
            send_sem=term_ssem.at[0, c], recv_sem=term_rsem.at[slot - 4, c],
            device_id=ahead, device_id_type=MESH,
        ).wait_recv()

    def add_term(into, slot, c):
        here = span(c)
        pool[into, here] = (pool[into, here].astype(F32) + pool[slot, here].astype(F32)).astype(BF16)

    def back_step(p):
        @pl.when((p >= 0) & (p < CHUNKS))
        def _():
            term_copy(1, p).start()

        c0 = p - 1 - 2 * inner

        @pl.when((c0 >= 0) & (c0 < CHUNKS))
        def _():
            term_wait(5, c0)

            @pl.when(inner == 1)
            def _():
                add_term(0, 5, c0)

            term_copy(0, c0).start()

        c2 = p - 2 - inner

        @pl.when((c2 >= 0) & (c2 < CHUNKS))
        def _():
            term_wait(6, c2)

            @pl.when(inner == 0)
            def _():
                add_term(1, 6, c2)

            term_copy(2, c2).start()

        c3 = p - 1 - inner

        @pl.when((c3 >= 0) & (c3 < CHUNKS))
        def _():
            term_wait(7, c3)

            @pl.when(inner == 1)
            def _():
                add_term(1, 7, c3)

            term_copy(3, c3).start()

    def compute(c):
        here = span(c)
        tok_wait(1, c)
        tok_wait(5, c)

        @pl.when(inner == 0)
        def _():
            tok_wait(4, c)

        first = 4 * (1 - inner)
        second = 2 + inner
        for n in range(2):
            v = nn(tok[here, half(n)], w[n, 0]) + nn(tok[here, half(1 - n)], w[n, 1])
            v = v + nn(recv[first, here, half(n)], w[n, 2]) + nn(recv[second, here, half(n)], w[n, 3])
            v = v + nn(recv[1, here, half(n)], w[n, 4]) + nn(recv[5, here, half(n)], w[n, 5])
            square = v * v
            t = jnp.tanh(SLOPE * (v + CUBE * (square * v)))
            outv[here, half(n)] = (0.5 * v * (1.0 + t)).astype(BF16)
            slope = 0.5 * (1.0 + t) + 0.5 * v * (1.0 - t * t) * (SLOPE * (1.0 + 3.0 * CUBE * square))
            delta[here, half(n)] = (cot[here, half(n)].astype(F32) * slope).astype(BF16)
        for b in (0, 3, 2, 1):
            for n in range(2):
                pool[b, here, half(n)] = nt(delta[here, half(n)], w[n, b + 2]).astype(BF16)
            if b == 0:
                @pl.when(inner == 0)
                def _():
                    term_copy(4, c).start()
            if b == 3:
                term_copy(5, c).start()
        for n in range(2):
            mid = nt(delta[here, half(n)], w[n, 0]).astype(BF16).astype(F32)
            side = nt(delta[here, half(1 - n)], w[1 - n, 1]).astype(BF16).astype(F32)
            acc[here, half(n)] = mid + side

    own(0)

    @pl.loop(0, CHUNKS + LAG)
    def _(i):
        own(i + 1)
        relay(0, 1, i - 3 + 2 * inner)
        relay(2, 2, i - 2 + inner)
        relay(3, 3, i - 3 + inner)

        @pl.when(i == LAG)
        def _():
            load_w.wait()
            load_cot.wait()

        @pl.when(i >= LAG)
        def _():
            compute(i - LAG)
            back_step(i - LAG - BACK)

    store_out = pltpu.make_async_copy(outv, out_hbm, store_sem.at[0])
    store_out.start()

    def core_copy(k):
        return pltpu.make_async_remote_copy(
            src_ref=other.at[k], dst_ref=crecv.at[k],
            send_sem=c_ssem.at[k], recv_sem=c_rsem.at[k],
            device_id=core_mate, device_id_type=MESH,
        )

    def rs_copy(k, j):
        return pltpu.make_async_remote_copy(
            src_ref=total.at[k, chip_of(j)], dst_ref=rsrecv.at[j - 1, k],
            send_sem=rs_ssem.at[j - 1, k], recv_sem=rs_rsem.at[j - 1, k],
            device_id=mate(j), device_id_type=MESH,
        )

    first = 4 * (1 - inner)
    second = 2 + inner

    def weight_grad(k):
        for n in range(2):
            if k == 0:
                left = tok[:, half(n)]
            elif k == 1:
                left = tok[:, half(1 - n)]
            else:
                left = recv[(first, second, 1, 5)[k - 2], :, half(n)]
            grad = tn(left, delta[:, half(n)])
            grad = grad.reshape(CHIPS, 2, BLK // 16, BLK)
            even, odd = grad[:, 0], grad[:, 1]
            mine[k, :, n] = jnp.where(core == 0, even, odd)
            other[k, :, n] = jnp.where(core == 0, odd, even).astype(BF16)
        core_copy(k).start()

    def pair_sum(k):
        core_copy(k).wait_recv()
        for q in range(CHIPS):
            both = mine[k, q] + crecv[k, q].astype(F32)
            mine[k, q] = both
            total[k, q] = both.astype(BF16)
        for j in range(1, CHIPS):
            rs_copy(k, j).start()

    todo = [(weight_grad, 0), (weight_grad, 1), (weight_grad, 2)]
    for k in range(PARTNERS):
        todo.append((pair_sum, k))
        if k + 3 < PARTNERS:
            todo.append((weight_grad, k + 3))
    steps = BACK + 3
    for t in range(steps):
        back_step(CHUNKS - BACK + t)
        for work, k in todo[t * len(todo) // steps : (t + 1) * len(todo) // steps]:
            work(k)

    @pl.loop(0, CHUNKS)
    def _(c):
        here = span(c)
        term_wait(4, c)
        term_wait(9, c)

        @pl.when(inner == 1)
        def _():
            term_wait(8, c)
            acc[here, :] += pool[8, here].astype(F32)

        result = acc[here, :] + pool[4, here].astype(F32) + pool[9, here].astype(F32)
        cot[here, :] = result.astype(BF16)

    store_ig = pltpu.make_async_copy(cot, ig_hbm, store_sem.at[1])
    store_ig.start()

    @pl.loop(0, PARTNERS)
    def _(k):
        for j in range(1, CHIPS):
            rs_copy(k, j).wait_recv()
        summed = mine[k, chip]
        for j in range(1, CHIPS):
            summed = summed + rsrecv[j - 1, k].astype(F32)
        for n in range(2):
            wgv[n, k] = summed[n]

    store_wg = pltpu.make_async_copy(wgv, wg_hbm, store_sem.at[2])
    store_wg.start()

    @pl.loop(0, CHUNKS)
    def _(c):
        for flow in (0, 1, 2, 3, 5):
            tok_copy(flow, c).wait_send()
            term_copy(flow, c).wait_send()

        @pl.when(inner == 1)
        def _():
            tok_copy(4, c).wait_send()

        @pl.when(inner == 0)
        def _():
            term_copy(4, c).wait_send()

    @pl.loop(0, PARTNERS)
    def _(k):
        core_copy(k).wait_send()
        for j in range(1, CHIPS):
            rs_copy(k, j).wait_send()

    store_out.wait()
    store_ig.wait()
    store_wg.wait()


def local(tokens, weight, cotangent):
    r, width = tokens.shape
    strip = BLK // 16
    dma = pltpu.SemaphoreType.DMA
    return pl.pallas_call(
        kernel,
        out_shape=(
            jax.ShapeDtypeStruct((r, width), BF16),
            jax.ShapeDtypeStruct((r, width), BF16),
            jax.ShapeDtypeStruct((2, PARTNERS, strip, BLK), F32),
        ),
        in_specs=[pl.BlockSpec(memory_space=pl.ANY)] * 3,
        out_specs=[pl.BlockSpec(memory_space=pl.ANY)] * 3,
        scratch_shapes=[
            pltpu.VMEM((r, width), BF16),
            pltpu.VMEM(weight.shape, BF16),
            pltpu.VMEM((r, width), BF16),
            pltpu.VMEM((FLOWS, r, width), BF16),
            pltpu.VMEM((r, width), BF16),
            pltpu.VMEM((r, width), BF16),
            pltpu.VMEM((r, width), F32),
            pltpu.VMEM((4 + FLOWS, r, width), BF16),
            pltpu.VMEM((PARTNERS, CHIPS, 2, strip, BLK), F32),
            pltpu.VMEM((PARTNERS, CHIPS, 2, strip, BLK), BF16),
            pltpu.VMEM((PARTNERS, CHIPS, 2, strip, BLK), BF16),
            pltpu.VMEM((PARTNERS, CHIPS, 2, strip, BLK), BF16),
            pltpu.VMEM((CHIPS - 1, PARTNERS, 2, strip, BLK), BF16),
            pltpu.VMEM((2, PARTNERS, strip, BLK), F32),
            dma((3,)),
            dma((3,)),
            dma((FLOWS, CHUNKS)),
            dma((FLOWS, CHUNKS)),
            dma((FLOWS, CHUNKS)),
            dma((FLOWS, CHUNKS)),
            dma((PARTNERS,)),
            dma((PARTNERS,)),
            dma((CHIPS - 1, PARTNERS)),
            dma((CHIPS - 1, PARTNERS)),
        ],
        compiler_params=pltpu.CompilerParams(
            collective_id=0, has_side_effects=True, vmem_limit_bytes=64_000_000
        ),
    )(tokens, weight, cotangent)


def solution(mesh):
    return jax.shard_map(
        local,
        mesh=mesh,
        in_specs=(P("dp", "feat"), P("feat", None, None, None), P("dp", "feat")),
        out_specs=(P("dp", "feat"), P("dp", "feat"), P("feat", None, "dp", None)),
        check_vma=False,
    )
```

```python
import functools

import jax
import jax.numpy as jnp
from jax import lax
from jax.experimental import pallas as pl
from jax.experimental.pallas import tpu as pltpu
from jax.sharding import PartitionSpec as P

F32 = jnp.float32
BF16 = jnp.bfloat16
MESH = pl.DeviceIdType.MESH
BLK = 512
PARTNERS = 6
CHUNKS = 16
HOP = 2
LAG = 8
SPREAD = 5
BACK = 8
FLOWS = 6
CHIPS = 8
SLOPE = 0.7978845608028654
CUBE = 0.044715


def flip(value, bit):
    return value + bit - 2 * bit * ((value // bit) % 2)


def nn(a, b):
    return lax.dot_general(a, b, (((1,), (0,)), ((), ())), preferred_element_type=F32)


def nt(a, b):
    return lax.dot_general(a, b, (((1,), (1,)), ((), ())), preferred_element_type=F32)


def tn(a, b):
    return lax.dot_general(a, b, (((0,), (0,)), ((), ())), preferred_element_type=F32)


def kernel(
    tok_hbm, w_hbm, cot_hbm, out_hbm, ig_hbm, wg_hbm,
    tok, w, cot, recv, delta, outv, acc, pool, mine, other, crecv, total, rsrecv, wgv,
    load_sem, store_sem, tok_ssem, tok_rsem, term_ssem, term_rsem, c_ssem, c_rsem, rs_ssem, rs_rsem,
):
    rows = tok.shape[0] // CHUNKS
    d = lax.axis_index("dp")
    f = lax.axis_index("feat")
    core = d % 2
    chip = d // 2
    y = chip // 2
    x_lo = chip % 2
    z = f % 8
    inner = (z + z // 2) % 2
    sgn = 1 - 2 * ((z // 2) % 2)

    def along(step):
        return (d, (f // 8) * 8 + (z + step + 8) % 8)

    ahead = along(sgn)
    behind = along(-sgn)
    across = (d, flip(f, 8))
    core_mate = (flip(d, 1), f)

    def chip_of(j):
        dy, dx = j // 2, j % 2
        return ((y + dy) % 4) * 2 + (x_lo + dx) % 2

    def mate(j):
        return (chip_of(j) * 2 + core, f)

    everyone = [ahead, behind, across, core_mate]
    barrier = pltpu.get_barrier_semaphore()
    for who in everyone:
        pl.semaphore_signal(barrier, inc=1, device_id=who, device_id_type=MESH)
    for j in range(1, CHIPS):
        pl.semaphore_signal(barrier, inc=1, device_id=mate(j), device_id_type=MESH)

    load_tok = pltpu.make_async_copy(tok_hbm, tok, load_sem.at[0])
    load_w = pltpu.make_async_copy(w_hbm, w, load_sem.at[1])
    load_cot = pltpu.make_async_copy(cot_hbm, cot, load_sem.at[2])
    load_tok.start()
    load_w.start()
    load_cot.start()
    pl.semaphore_wait(barrier, len(everyone) + CHIPS - 1)
    load_tok.wait()

    def span(c):
        return pl.ds(pl.multiple_of(c * rows, rows), rows)

    def pair_span(q):
        return pl.ds(pl.multiple_of(q * 2 * rows, 2 * rows), 2 * rows)

    def half(n):
        return pl.ds(n * BLK, BLK)

    def tok_copy(flow, c):
        source, slot, to = (
            (tok.at[span(c)], 2 * inner, ahead),
            (recv.at[0, span(c)], 2 * inner + 1, ahead),
            (recv.at[2, span(c)], 2 * inner, behind),
            (recv.at[3, span(c)], 2 * inner + 1, behind),
            (tok.at[span(c)], 4, behind),
            (tok.at[span(c)], 5, across),
        )[flow]
        return pltpu.make_async_remote_copy(
            src_ref=source, dst_ref=recv.at[slot, span(c)],
            send_sem=tok_ssem.at[flow, c], recv_sem=tok_rsem.at[slot, c],
            device_id=to, device_id_type=MESH,
        )

    def tok_wait(slot, c):
        pltpu.make_async_remote_copy(
            src_ref=recv.at[slot, span(c)], dst_ref=recv.at[slot, span(c)],
            send_sem=tok_ssem.at[0, c], recv_sem=tok_rsem.at[slot, c],
            device_id=ahead, device_id_type=MESH,
        ).wait_recv()

    def own(c):
        @pl.when(c < CHUNKS)
        def _():
            tok_copy(0, c).start()
            tok_copy(5, c).start()

            @pl.when(inner == 1)
            def _():
                tok_copy(4, c).start()

    def relay(slot, flow, c):
        @pl.when((c >= 0) & (c < CHUNKS))
        def _():
            tok_wait(slot, c)
            tok_copy(flow, c).start()

    low = 4 + 2 * (1 - inner)

    def term_copy(flow, c):
        source, slot, to = (
            (5 * (1 - inner), low, behind),
            (2, low + 1, behind),
            (1 + 5 * inner, low, ahead),
            (1 + 6 * (1 - inner), low + 1, ahead),
            (0, 8, ahead),
            (3, 9, across),
        )[flow]
        return pltpu.make_async_remote_copy(
            src_ref=pool.at[source, span(c)], dst_ref=pool.at[slot, span(c)],
            send_sem=term_ssem.at[flow, c], recv_sem=term_rsem.at[slot - 4, c],
            device_id=to, device_id_type=MESH,
        )

    def term_wait(slot, c):
        pltpu.make_async_remote_copy(
            src_ref=pool.at[slot, span(c)], dst_ref=pool.at[slot, span(c)],
            send_sem=term_ssem.at[0, c], recv_sem=term_rsem.at[slot - 4, c],
            device_id=ahead, device_id_type=MESH,
        ).wait_recv()

    def add_term(into, slot, c):
        here = span(c)
        pool[into, here] = (pool[into, here].astype(F32) + pool[slot, here].astype(F32)).astype(BF16)

    def back_step(p):
        @pl.when((p >= 0) & (p < CHUNKS))
        def _():
            term_copy(1, p).start()

        c0 = p - HOP * (1 + 2 * inner)

        @pl.when((c0 >= 0) & (c0 < CHUNKS))
        def _():
            term_wait(5, c0)

            @pl.when(inner == 1)
            def _():
                add_term(0, 5, c0)

            term_copy(0, c0).start()

        c2 = p - HOP * (2 + inner)

        @pl.when((c2 >= 0) & (c2 < CHUNKS))
        def _():
            term_wait(6, c2)

            @pl.when(inner == 0)
            def _():
                add_term(1, 6, c2)

            term_copy(2, c2).start()

        c3 = p - HOP * (1 + inner)

        @pl.when((c3 >= 0) & (c3 < CHUNKS))
        def _():
            term_wait(7, c3)

            @pl.when(inner == 1)
            def _():
                add_term(1, 7, c3)

            term_copy(3, c3).start()

    def forward(q):
        here = pair_span(q)
        for c in (2 * q, 2 * q + 1):
            tok_wait(1, c)
            tok_wait(5, c)

        @pl.when(inner == 0)
        def _():
            tok_wait(4, 2 * q)
            tok_wait(4, 2 * q + 1)

        first = 4 * (1 - inner)
        second = 2 + inner
        for n in range(2):
            v = nn(tok[here, half(n)], w[n, 0]) + nn(tok[here, half(1 - n)], w[n, 1])
            v = v + nn(recv[first, here, half(n)], w[n, 2]) + nn(recv[second, here, half(n)], w[n, 3])
            v = v + nn(recv[1, here, half(n)], w[n, 4]) + nn(recv[5, here, half(n)], w[n, 5])
            square = v * v
            t = jnp.tanh(SLOPE * (v + CUBE * (square * v)))
            outv[here, half(n)] = (0.5 * v * (1.0 + t)).astype(BF16)
            slope = 0.5 * (1.0 + t) + 0.5 * v * (1.0 - t * t) * (SLOPE * (1.0 + 3.0 * CUBE * square))
            delta[here, half(n)] = (cot[here, half(n)].astype(F32) * slope).astype(BF16)

    def backward(q):
        here = pair_span(q)
        for b in (0, 3, 2, 1):
            for n in range(2):
                pool[b, here, half(n)] = nt(delta[here, half(n)], w[n, b + 2]).astype(BF16)
            if b == 0:
                @pl.when(inner == 0)
                def _():
                    term_copy(4, 2 * q).start()
                    term_copy(4, 2 * q + 1).start()
            if b == 3:
                term_copy(5, 2 * q).start()
                term_copy(5, 2 * q + 1).start()
        for n in range(2):
            mid = nt(delta[here, half(n)], w[n, 0]).astype(BF16).astype(F32)
            side = nt(delta[here, half(1 - n)], w[1 - n, 1]).astype(BF16).astype(F32)
            acc[here, half(n)] = mid + side

    own(0)

    @pl.loop(0, CHUNKS + LAG)
    def _(i):
        own(i + 1)
        relay(0, 1, i - HOP * (3 - 2 * inner))
        relay(2, 2, i - HOP * (2 - inner))
        relay(3, 3, i - HOP * (3 - inner))
        q = i - LAG

        @pl.when(q == 0)
        def _():
            load_w.wait()
            load_cot.wait()

        @pl.when((q >= 0) & (q % 2 == 0))
        def _():
            forward(q // 2)

        @pl.when((q >= 0) & (q % 2 == 1))
        def _():
            backward(q // 2)

        back_step(q - 1 - BACK)

    store_out = pltpu.make_async_copy(outv, out_hbm, store_sem.at[0])
    store_out.start()

    def core_copy(k):
        return pltpu.make_async_remote_copy(
            src_ref=other.at[k], dst_ref=crecv.at[k],
            send_sem=c_ssem.at[k], recv_sem=c_rsem.at[k],
            device_id=core_mate, device_id_type=MESH,
        )

    def rs_copy(k, j):
        return pltpu.make_async_remote_copy(
            src_ref=total.at[k, chip_of(j)], dst_ref=rsrecv.at[j - 1, k],
            send_sem=rs_ssem.at[j - 1, k], recv_sem=rs_rsem.at[j - 1, k],
            device_id=mate(j), device_id_type=MESH,
        )

    first = 4 * (1 - inner)
    second = 2 + inner

    def weight_grad(k):
        for n in range(2):
            if k == 0:
                left = tok[:, half(n)]
            elif k == 1:
                left = tok[:, half(1 - n)]
            else:
                left = recv[(first, second, 1, 5)[k - 2], :, half(n)]
            grad = tn(left, delta[:, half(n)])
            grad = grad.reshape(CHIPS, 2, BLK // 16, BLK)
            even, odd = grad[:, 0], grad[:, 1]
            mine[k, :, n] = jnp.where(core == 0, even, odd)
            other[k, :, n] = jnp.where(core == 0, odd, even).astype(BF16)
        core_copy(k).start()

    def pair_sum(k):
        core_copy(k).wait_recv()
        for q in range(CHIPS):
            both = mine[k, q] + crecv[k, q].astype(F32)
            mine[k, q] = both
            total[k, q] = both.astype(BF16)
        for j in range(1, CHIPS):
            rs_copy(k, j).start()

    todo = [(weight_grad, 0), (weight_grad, 1), (weight_grad, 2)]
    for k in range(PARTNERS):
        todo.append((pair_sum, k))
        if k + 3 < PARTNERS:
            todo.append((weight_grad, k + 3))
    for t in range(BACK + 1 + 3 * HOP):
        back_step(CHUNKS - 1 - BACK + t)
        for work, k in todo[t * len(todo) // SPREAD : (t + 1) * len(todo) // SPREAD]:
            work(k)

    @pl.loop(0, CHUNKS)
    def _(c):
        here = span(c)
        term_wait(4, c)
        term_wait(9, c)

        @pl.when(inner == 1)
        def _():
            term_wait(8, c)
            acc[here, :] += pool[8, here].astype(F32)

        result = acc[here, :] + pool[4, here].astype(F32) + pool[9, here].astype(F32)
        cot[here, :] = result.astype(BF16)

    store_ig = pltpu.make_async_copy(cot, ig_hbm, store_sem.at[1])
    store_ig.start()

    @pl.loop(0, PARTNERS)
    def _(k):
        for j in range(1, CHIPS):
            rs_copy(k, j).wait_recv()
        summed = mine[k, chip]
        for j in range(1, CHIPS):
            summed = summed + rsrecv[j - 1, k].astype(F32)
        for n in range(2):
            wgv[n, k] = summed[n]

    store_wg = pltpu.make_async_copy(wgv, wg_hbm, store_sem.at[2])
    store_wg.start()

    @pl.loop(0, CHUNKS)
    def _(c):
        for flow in (0, 1, 2, 3, 5):
            tok_copy(flow, c).wait_send()
            term_copy(flow, c).wait_send()

        @pl.when(inner == 1)
        def _():
            tok_copy(4, c).wait_send()

        @pl.when(inner == 0)
        def _():
            term_copy(4, c).wait_send()

    @pl.loop(0, PARTNERS)
    def _(k):
        core_copy(k).wait_send()
        for j in range(1, CHIPS):
            rs_copy(k, j).wait_send()

    store_out.wait()
    store_ig.wait()
    store_wg.wait()


def local(tokens, weight, cotangent):
    r, width = tokens.shape
    strip = BLK // 16
    dma = pltpu.SemaphoreType.DMA
    return pl.pallas_call(
        kernel,
        out_shape=(
            jax.ShapeDtypeStruct((r, width), BF16),
            jax.ShapeDtypeStruct((r, width), BF16),
            jax.ShapeDtypeStruct((2, PARTNERS, strip, BLK), F32),
        ),
        in_specs=[pl.BlockSpec(memory_space=pl.ANY)] * 3,
        out_specs=[pl.BlockSpec(memory_space=pl.ANY)] * 3,
        scratch_shapes=[
            pltpu.VMEM((r, width), BF16),
            pltpu.VMEM(weight.shape, BF16),
            pltpu.VMEM((r, width), BF16),
            pltpu.VMEM((FLOWS, r, width), BF16),
            pltpu.VMEM((r, width), BF16),
            pltpu.VMEM((r, width), BF16),
            pltpu.VMEM((r, width), F32),
            pltpu.VMEM((4 + FLOWS, r, width), BF16),
            pltpu.VMEM((PARTNERS, CHIPS, 2, strip, BLK), F32),
            pltpu.VMEM((PARTNERS, CHIPS, 2, strip, BLK), BF16),
            pltpu.VMEM((PARTNERS, CHIPS, 2, strip, BLK), BF16),
            pltpu.VMEM((PARTNERS, CHIPS, 2, strip, BLK), BF16),
            pltpu.VMEM((CHIPS - 1, PARTNERS, 2, strip, BLK), BF16),
            pltpu.VMEM((2, PARTNERS, strip, BLK), F32),
            dma((3,)),
            dma((3,)),
            dma((FLOWS, CHUNKS)),
            dma((FLOWS, CHUNKS)),
            dma((FLOWS, CHUNKS)),
            dma((FLOWS, CHUNKS)),
            dma((PARTNERS,)),
            dma((PARTNERS,)),
            dma((CHIPS - 1, PARTNERS)),
            dma((CHIPS - 1, PARTNERS)),
        ],
        compiler_params=pltpu.CompilerParams(
            collective_id=0, has_side_effects=True, vmem_limit_bytes=64_000_000
        ),
    )(tokens, weight, cotangent)


def solution(mesh):
    return jax.shard_map(
        local,
        mesh=mesh,
        in_specs=(P("dp", "feat"), P("feat", None, None, None), P("dp", "feat")),
        out_specs=(P("dp", "feat"), P("dp", "feat"), P("feat", None, "dp", None)),
        check_vma=False,
    )
```

```python
import functools

import jax
import jax.numpy as jnp
from jax import lax
from jax.experimental import pallas as pl
from jax.experimental.pallas import tpu as pltpu
from jax.sharding import PartitionSpec as P

F32 = jnp.float32
BF16 = jnp.bfloat16
MESH = pl.DeviceIdType.MESH
BLK = 512
PARTNERS = 6
CHUNKS = 16
HOP = 2
LAG = 8
LAST = 4
SPREAD = 5
EARLY = 6
BACK = 10
FLOWS = 6
CHIPS = 8
SLOPE = 0.7978845608028654
CUBE = 0.044715


def flip(value, bit):
    return value + bit - 2 * bit * ((value // bit) % 2)


def nn(a, b):
    return lax.dot_general(a, b, (((1,), (0,)), ((), ())), preferred_element_type=F32)


def nt(a, b):
    return lax.dot_general(a, b, (((1,), (1,)), ((), ())), preferred_element_type=F32)


def tn(a, b):
    return lax.dot_general(a, b, (((0,), (0,)), ((), ())), preferred_element_type=F32)


def kernel(
    tok_hbm, w_hbm, cot_hbm, out_hbm, ig_hbm, wg_hbm,
    tok, w, cot, recv, delta, outv, acc, pool, mine, other, crecv, total, rsrecv, wgv,
    load_sem, store_sem, tok_ssem, tok_rsem, term_ssem, term_rsem, c_ssem, c_rsem, rs_ssem, rs_rsem,
):
    rows = tok.shape[0] // CHUNKS
    d = lax.axis_index("dp")
    f = lax.axis_index("feat")
    core = d % 2
    chip = d // 2
    y = chip // 2
    x_lo = chip % 2
    z = f % 8
    inner = (z + z // 2) % 2
    sgn = 1 - 2 * ((z // 2) % 2)

    def along(step):
        return (d, (f // 8) * 8 + (z + step + 8) % 8)

    ahead = along(sgn)
    behind = along(-sgn)
    across = (d, flip(f, 8))
    core_mate = (flip(d, 1), f)

    def chip_of(j):
        dy, dx = j // 2, j % 2
        return ((y + dy) % 4) * 2 + (x_lo + dx) % 2

    def mate(j):
        return (chip_of(j) * 2 + core, f)

    everyone = [ahead, behind, across, core_mate]
    barrier = pltpu.get_barrier_semaphore()
    for who in everyone:
        pl.semaphore_signal(barrier, inc=1, device_id=who, device_id_type=MESH)
    for j in range(1, CHIPS):
        pl.semaphore_signal(barrier, inc=1, device_id=mate(j), device_id_type=MESH)

    load_tok = pltpu.make_async_copy(tok_hbm, tok, load_sem.at[0])
    load_w = pltpu.make_async_copy(w_hbm, w, load_sem.at[1])
    load_cot = pltpu.make_async_copy(cot_hbm, cot, load_sem.at[2])
    load_tok.start()
    load_w.start()
    load_cot.start()
    pl.semaphore_wait(barrier, len(everyone) + CHIPS - 1)
    load_tok.wait()

    def span(c):
        return pl.ds(pl.multiple_of(c * rows, rows), rows)

    def pair_span(q):
        return pl.ds(pl.multiple_of(q * 2 * rows, 2 * rows), 2 * rows)

    def half(n):
        return pl.ds(n * BLK, BLK)

    def tok_copy(flow, c):
        source, slot, to = (
            (tok.at[span(c)], 2 * inner, ahead),
            (recv.at[0, span(c)], 2 * inner + 1, ahead),
            (recv.at[2, span(c)], 2 * inner, behind),
            (recv.at[3, span(c)], 2 * inner + 1, behind),
            (tok.at[span(c)], 4, behind),
            (tok.at[span(c)], 5, across),
        )[flow]
        return pltpu.make_async_remote_copy(
            src_ref=source, dst_ref=recv.at[slot, span(c)],
            send_sem=tok_ssem.at[flow, c], recv_sem=tok_rsem.at[slot, c],
            device_id=to, device_id_type=MESH,
        )

    def tok_wait(slot, c):
        pltpu.make_async_remote_copy(
            src_ref=recv.at[slot, span(c)], dst_ref=recv.at[slot, span(c)],
            send_sem=tok_ssem.at[0, c], recv_sem=tok_rsem.at[slot, c],
            device_id=ahead, device_id_type=MESH,
        ).wait_recv()

    def own(c):
        @pl.when(c < CHUNKS)
        def _():
            tok_copy(0, c).start()
            tok_copy(5, c).start()

            @pl.when(inner == 1)
            def _():
                tok_copy(4, c).start()

    def relay(slot, flow, c):
        @pl.when((c >= 0) & (c < CHUNKS))
        def _():
            tok_wait(slot, c)
            tok_copy(flow, c).start()

    low = 4 + 2 * (1 - inner)

    def term_copy(flow, c):
        source, slot, to = (
            (5 * (1 - inner), low, behind),
            (2, low + 1, behind),
            (1 + 5 * inner, low, ahead),
            (1 + 6 * (1 - inner), low + 1, ahead),
            (0, 8, ahead),
            (3, 9, across),
        )[flow]
        return pltpu.make_async_remote_copy(
            src_ref=pool.at[source, span(c)], dst_ref=pool.at[slot, span(c)],
            send_sem=term_ssem.at[flow, c], recv_sem=term_rsem.at[slot - 4, c],
            device_id=to, device_id_type=MESH,
        )

    def term_wait(slot, c):
        pltpu.make_async_remote_copy(
            src_ref=pool.at[slot, span(c)], dst_ref=pool.at[slot, span(c)],
            send_sem=term_ssem.at[0, c], recv_sem=term_rsem.at[slot - 4, c],
            device_id=ahead, device_id_type=MESH,
        ).wait_recv()

    def add_term(into, slot, c):
        here = span(c)
        pool[into, here] = (pool[into, here].astype(F32) + pool[slot, here].astype(F32)).astype(BF16)

    def back_step(p):
        c1 = p + EARLY * (1 - inner)

        @pl.when((c1 >= 0) & (c1 < CHUNKS))
        def _():
            term_copy(1, c1).start()

        c0 = p - HOP * (1 + 2 * inner) + EARLY * inner

        @pl.when((c0 >= 0) & (c0 < CHUNKS))
        def _():
            term_wait(5, c0)

            @pl.when(inner == 1)
            def _():
                add_term(0, 5, c0)

            term_copy(0, c0).start()

        c2 = p - HOP * (2 + inner)

        @pl.when((c2 >= 0) & (c2 < CHUNKS))
        def _():
            term_wait(6, c2)

            @pl.when(inner == 0)
            def _():
                add_term(1, 6, c2)

            term_copy(2, c2).start()

        c3 = p - HOP * (1 + inner) + EARLY

        @pl.when((c3 >= 0) & (c3 < CHUNKS))
        def _():
            term_wait(7, c3)

            @pl.when(inner == 1)
            def _():
                add_term(1, 7, c3)

            term_copy(3, c3).start()

    def forward(q):
        here = pair_span(q)
        for c in (2 * q, 2 * q + 1):
            tok_wait(1, c)
            tok_wait(5, c)

        @pl.when(inner == 0)
        def _():
            tok_wait(4, 2 * q)
            tok_wait(4, 2 * q + 1)

        first = 4 * (1 - inner)
        second = 2 + inner
        for n in range(2):
            v = nn(tok[here, half(n)], w[n, 0]) + nn(tok[here, half(1 - n)], w[n, 1])
            v = v + nn(recv[first, here, half(n)], w[n, 2]) + nn(recv[second, here, half(n)], w[n, 3])
            v = v + nn(recv[1, here, half(n)], w[n, 4]) + nn(recv[5, here, half(n)], w[n, 5])
            square = v * v
            t = jnp.tanh(SLOPE * (v + CUBE * (square * v)))
            outv[here, half(n)] = (0.5 * v * (1.0 + t)).astype(BF16)
            slope = 0.5 * (1.0 + t) + 0.5 * v * (1.0 - t * t) * (SLOPE * (1.0 + 3.0 * CUBE * square))
            delta[here, half(n)] = (cot[here, half(n)].astype(F32) * slope).astype(BF16)

    def backward(q):
        here = pair_span(q)
        for b in (0, 3, 2, 1):
            for n in range(2):
                pool[b, here, half(n)] = nt(delta[here, half(n)], w[n, b + 2]).astype(BF16)
            if b == 0:
                @pl.when(inner == 0)
                def _():
                    term_copy(4, 2 * q).start()
                    term_copy(4, 2 * q + 1).start()
            if b == 3:
                term_copy(5, 2 * q).start()
                term_copy(5, 2 * q + 1).start()
        for n in range(2):
            mid = nt(delta[here, half(n)], w[n, 0]).astype(BF16).astype(F32)
            side = nt(delta[here, half(1 - n)], w[1 - n, 1]).astype(BF16).astype(F32)
            acc[here, half(n)] = mid + side

    own(0)

    @pl.loop(0, CHUNKS + LAG)
    def _(i):
        own(i + 1)
        relay(0, 1, i - HOP * (3 - 2 * inner))
        relay(2, 2, i - HOP * (2 - inner))
        relay(3, 3, i - HOP * (3 - inner))
        q = i - LAG

        @pl.when(q == 0)
        def _():
            load_w.wait()
            load_cot.wait()

        @pl.when((q >= 0) & (q % 2 == 0))
        def _():
            forward(q // 2)

        @pl.when((q >= 0) & (q % 2 == 1))
        def _():
            backward(q // 2)

        back_step(q - 1 - BACK)

    store_out = pltpu.make_async_copy(outv, out_hbm, store_sem.at[0])
    store_out.start()

    def core_copy(k):
        return pltpu.make_async_remote_copy(
            src_ref=other.at[k], dst_ref=crecv.at[k],
            send_sem=c_ssem.at[k], recv_sem=c_rsem.at[k],
            device_id=core_mate, device_id_type=MESH,
        )

    def rs_copy(k, j):
        return pltpu.make_async_remote_copy(
            src_ref=total.at[k, chip_of(j)], dst_ref=rsrecv.at[j - 1, k],
            send_sem=rs_ssem.at[j - 1, k], recv_sem=rs_rsem.at[j - 1, k],
            device_id=mate(j), device_id_type=MESH,
        )

    first = 4 * (1 - inner)
    second = 2 + inner

    def weight_grad(k):
        for n in range(2):
            if k == 0:
                left = tok[:, half(n)]
            elif k == 1:
                left = tok[:, half(1 - n)]
            else:
                left = recv[(first, second, 1, 5)[k - 2], :, half(n)]
            grad = tn(left, delta[:, half(n)])
            grad = grad.reshape(CHIPS, 2, BLK // 16, BLK)
            even, odd = grad[:, 0], grad[:, 1]
            mine[k, :, n] = jnp.where(core == 0, even, odd)
            other[k, :, n] = jnp.where(core == 0, odd, even).astype(BF16)
        core_copy(k).start()

    def pair_sum(k):
        core_copy(k).wait_recv()
        for q in range(CHIPS):
            total[k, q] = (mine[k, q] + crecv[k, q].astype(F32)).astype(BF16)
        for j in range(1, CHIPS):
            rs_copy(k, j).start()

    todo = [(weight_grad, 0), (weight_grad, 1), (weight_grad, 2)]
    for k in range(PARTNERS):
        todo.append((pair_sum, k))
        if k + 3 < PARTNERS:
            todo.append((weight_grad, k + 3))
    for t in range(BACK + 1 + 3 * HOP):
        back_step(CHUNKS - 1 - BACK + t)
        for work, k in todo[t * len(todo) // SPREAD : (t + 1) * len(todo) // SPREAD]:
            work(k)

    def gather_terms(c):
        here = span(c)
        term_wait(4, c)
        term_wait(9, c)

        @pl.when(inner == 1)
        def _():
            term_wait(8, c)
            acc[here, :] += pool[8, here].astype(F32)

        result = acc[here, :] + pool[4, here].astype(F32) + pool[9, here].astype(F32)
        cot[here, :] = result.astype(BF16)

    def store_ig(c, size):
        part = pl.ds(c * rows, size * rows)
        return pltpu.make_async_copy(cot.at[part], ig_hbm.at[part], store_sem.at[1 if c == 0 else 3])

    pl.loop(0, CHUNKS - LAST)(gather_terms)
    store_ig(0, CHUNKS - LAST).start()

    @pl.loop(0, PARTNERS)
    def _(k):
        for j in range(1, CHIPS):
            rs_copy(k, j).wait_recv()
        summed = mine[k, chip] + crecv[k, chip].astype(F32)
        for j in range(1, CHIPS):
            summed = summed + rsrecv[j - 1, k].astype(F32)
        for n in range(2):
            wgv[n, k] = summed[n]

    store_wg = pltpu.make_async_copy(wgv, wg_hbm, store_sem.at[2])
    store_wg.start()
    pl.loop(CHUNKS - LAST, CHUNKS)(gather_terms)
    store_ig(CHUNKS - LAST, LAST).start()

    @pl.loop(0, CHUNKS)
    def _(c):
        for flow in (0, 1, 2, 3, 5):
            tok_copy(flow, c).wait_send()
            term_copy(flow, c).wait_send()

        @pl.when(inner == 1)
        def _():
            tok_copy(4, c).wait_send()

        @pl.when(inner == 0)
        def _():
            term_copy(4, c).wait_send()

    @pl.loop(0, PARTNERS)
    def _(k):
        core_copy(k).wait_send()
        for j in range(1, CHIPS):
            rs_copy(k, j).wait_send()

    store_out.wait()
    store_ig(0, CHUNKS - LAST).wait()
    store_ig(CHUNKS - LAST, LAST).wait()
    store_wg.wait()


def place(*refs):
    arrays, outs, buffers, sems = refs[:3], refs[3:6], refs[6:9], refs[9]
    reads = [pltpu.make_async_copy(a, b, sems.at[0, i]) for i, (a, b) in enumerate(zip(arrays, buffers))]
    writes = [pltpu.make_async_copy(b, o, sems.at[1, i]) for i, (b, o) in enumerate(zip(buffers, outs))]
    for read in reads:
        read.start()
    for read, write in zip(reads, writes):
        read.wait()
        write.start()
    for write in writes:
        write.wait()


def local(tokens, weight, cotangent):
    r, width = tokens.shape
    strip = BLK // 16
    dma = pltpu.SemaphoreType.DMA
    results = pl.pallas_call(
        kernel,
        out_shape=(
            jax.ShapeDtypeStruct((r, width), BF16),
            jax.ShapeDtypeStruct((r, width), BF16),
            jax.ShapeDtypeStruct((2, PARTNERS, strip, BLK), F32),
        ),
        in_specs=[pl.BlockSpec(memory_space=pl.ANY)] * 3,
        out_specs=[pl.BlockSpec(memory_space=pl.ANY)] * 3,
        scratch_shapes=[
            pltpu.VMEM((r, width), BF16),
            pltpu.VMEM(weight.shape, BF16),
            pltpu.VMEM((r, width), BF16),
            pltpu.VMEM((FLOWS, r, width), BF16),
            pltpu.VMEM((r, width), BF16),
            pltpu.VMEM((r, width), BF16),
            pltpu.VMEM((r, width), F32),
            pltpu.VMEM((4 + FLOWS, r, width), BF16),
            pltpu.VMEM((PARTNERS, CHIPS, 2, strip, BLK), F32),
            pltpu.VMEM((PARTNERS, CHIPS, 2, strip, BLK), BF16),
            pltpu.VMEM((PARTNERS, CHIPS, 2, strip, BLK), BF16),
            pltpu.VMEM((PARTNERS, CHIPS, 2, strip, BLK), BF16),
            pltpu.VMEM((CHIPS - 1, PARTNERS, 2, strip, BLK), BF16),
            pltpu.VMEM((2, PARTNERS, strip, BLK), F32),
            dma((3,)),
            dma((4,)),
            dma((FLOWS, CHUNKS)),
            dma((FLOWS, CHUNKS)),
            dma((FLOWS, CHUNKS)),
            dma((FLOWS, CHUNKS)),
            dma((PARTNERS,)),
            dma((PARTNERS,)),
            dma((CHIPS - 1, PARTNERS)),
            dma((CHIPS - 1, PARTNERS)),
        ],
        compiler_params=pltpu.CompilerParams(
            collective_id=0, has_side_effects=True, vmem_limit_bytes=64_000_000
        ),
    )(tokens, weight, cotangent)
    return pl.pallas_call(
        place,
        out_shape=tuple(jax.ShapeDtypeStruct(a.shape, a.dtype) for a in results),
        in_specs=[pl.BlockSpec(memory_space=pl.ANY)] * 3,
        out_specs=[pl.BlockSpec(memory_space=pl.ANY)] * 3,
        scratch_shapes=[pltpu.VMEM(a.shape, a.dtype) for a in results] + [dma((2, 3))],
    )(*results)


def solution(mesh):
    return jax.shard_map(
        local,
        mesh=mesh,
        in_specs=(P("dp", "feat"), P("feat", None, None, None), P("dp", "feat")),
        out_specs=(P("dp", "feat"), P("dp", "feat"), P("feat", None, "dp", None)),
        check_vma=False,
    )
```

```python
import functools

import jax
import jax.numpy as jnp
from jax import lax
from jax.experimental import pallas as pl
from jax.experimental.pallas import tpu as pltpu
from jax.sharding import PartitionSpec as P

F32 = jnp.float32
BF16 = jnp.bfloat16
MESH = pl.DeviceIdType.MESH
BLK = 512
PARTNERS = 6
CHUNKS = 16
HOP = 2
LAG = 8
LAST = 4
SPREAD = 5
EARLY = 6
BACK = 10
FLOWS = 6
CHIPS = 8
SLOPE = 0.7978845608028654
CUBE = 0.044715


def flip(value, bit):
    return value + bit - 2 * bit * ((value // bit) % 2)


def nn(a, b):
    return lax.dot_general(a, b, (((1,), (0,)), ((), ())), preferred_element_type=F32)


def nt(a, b):
    return lax.dot_general(a, b, (((1,), (1,)), ((), ())), preferred_element_type=F32)


def tn(a, b):
    return lax.dot_general(a, b, (((0,), (0,)), ((), ())), preferred_element_type=F32)


def kernel(
    tok_hbm, w_hbm, cot_hbm, outv, ig, wgv,
    tok, w, cot, recv, delta, acc, pool, mine, other, crecv, total, rsrecv,
    load_sem, tok_ssem, tok_rsem, term_ssem, term_rsem, c_ssem, c_rsem, rs_ssem, rs_rsem,
):
    rows = tok.shape[0] // CHUNKS
    d = lax.axis_index("dp")
    f = lax.axis_index("feat")
    core = d % 2
    chip = d // 2
    y = chip // 2
    x_lo = chip % 2
    z = f % 8
    inner = (z + z // 2) % 2
    sgn = 1 - 2 * ((z // 2) % 2)

    def along(step):
        return (d, (f // 8) * 8 + (z + step + 8) % 8)

    ahead = along(sgn)
    behind = along(-sgn)
    across = (d, flip(f, 8))
    core_mate = (flip(d, 1), f)

    def chip_of(j):
        dy, dx = j // 2, j % 2
        return ((y + dy) % 4) * 2 + (x_lo + dx) % 2

    def mate(j):
        return (chip_of(j) * 2 + core, f)

    everyone = [ahead, behind, across, core_mate]
    barrier = pltpu.get_barrier_semaphore()
    for who in everyone:
        pl.semaphore_signal(barrier, inc=1, device_id=who, device_id_type=MESH)
    for j in range(1, CHIPS):
        pl.semaphore_signal(barrier, inc=1, device_id=mate(j), device_id_type=MESH)

    load_tok = pltpu.make_async_copy(tok_hbm, tok, load_sem.at[0])
    load_w = pltpu.make_async_copy(w_hbm, w, load_sem.at[1])
    load_cot = pltpu.make_async_copy(cot_hbm, cot, load_sem.at[2])
    load_tok.start()
    load_w.start()
    load_cot.start()
    pl.semaphore_wait(barrier, len(everyone) + CHIPS - 1)
    load_tok.wait()

    def span(c):
        return pl.ds(pl.multiple_of(c * rows, rows), rows)

    def pair_span(q):
        return pl.ds(pl.multiple_of(q * 2 * rows, 2 * rows), 2 * rows)

    def half(n):
        return pl.ds(n * BLK, BLK)

    def tok_copy(flow, c):
        source, slot, to = (
            (tok.at[span(c)], 2 * inner, ahead),
            (recv.at[0, span(c)], 2 * inner + 1, ahead),
            (recv.at[2, span(c)], 2 * inner, behind),
            (recv.at[3, span(c)], 2 * inner + 1, behind),
            (tok.at[span(c)], 4, behind),
            (tok.at[span(c)], 5, across),
        )[flow]
        return pltpu.make_async_remote_copy(
            src_ref=source, dst_ref=recv.at[slot, span(c)],
            send_sem=tok_ssem.at[flow, c], recv_sem=tok_rsem.at[slot, c],
            device_id=to, device_id_type=MESH,
        )

    def tok_wait(slot, c):
        pltpu.make_async_remote_copy(
            src_ref=recv.at[slot, span(c)], dst_ref=recv.at[slot, span(c)],
            send_sem=tok_ssem.at[0, c], recv_sem=tok_rsem.at[slot, c],
            device_id=ahead, device_id_type=MESH,
        ).wait_recv()

    def own(c):
        @pl.when(c < CHUNKS)
        def _():
            tok_copy(0, c).start()
            tok_copy(5, c).start()

            @pl.when(inner == 1)
            def _():
                tok_copy(4, c).start()

    def relay(slot, flow, c):
        @pl.when((c >= 0) & (c < CHUNKS))
        def _():
            tok_wait(slot, c)
            tok_copy(flow, c).start()

    low = 4 + 2 * (1 - inner)

    def term_copy(flow, c):
        source, slot, to = (
            (5 * (1 - inner), low, behind),
            (2, low + 1, behind),
            (1 + 5 * inner, low, ahead),
            (1 + 6 * (1 - inner), low + 1, ahead),
            (0, 8, ahead),
            (3, 9, across),
        )[flow]
        return pltpu.make_async_remote_copy(
            src_ref=pool.at[source, span(c)], dst_ref=pool.at[slot, span(c)],
            send_sem=term_ssem.at[flow, c], recv_sem=term_rsem.at[slot - 4, c],
            device_id=to, device_id_type=MESH,
        )

    def term_wait(slot, c):
        pltpu.make_async_remote_copy(
            src_ref=pool.at[slot, span(c)], dst_ref=pool.at[slot, span(c)],
            send_sem=term_ssem.at[0, c], recv_sem=term_rsem.at[slot - 4, c],
            device_id=ahead, device_id_type=MESH,
        ).wait_recv()

    def add_term(into, slot, c):
        here = span(c)
        pool[into, here] = (pool[into, here].astype(F32) + pool[slot, here].astype(F32)).astype(BF16)

    def back_step(p):
        c1 = p + EARLY * (1 - inner)

        @pl.when((c1 >= 0) & (c1 < CHUNKS))
        def _():
            term_copy(1, c1).start()

        c0 = p - HOP * (1 + 2 * inner) + EARLY * inner

        @pl.when((c0 >= 0) & (c0 < CHUNKS))
        def _():
            term_wait(5, c0)

            @pl.when(inner == 1)
            def _():
                add_term(0, 5, c0)

            term_copy(0, c0).start()

        c2 = p - HOP * (2 + inner)

        @pl.when((c2 >= 0) & (c2 < CHUNKS))
        def _():
            term_wait(6, c2)

            @pl.when(inner == 0)
            def _():
                add_term(1, 6, c2)

            term_copy(2, c2).start()

        c3 = p - HOP * (1 + inner) + EARLY

        @pl.when((c3 >= 0) & (c3 < CHUNKS))
        def _():
            term_wait(7, c3)

            @pl.when(inner == 1)
            def _():
                add_term(1, 7, c3)

            term_copy(3, c3).start()

    def forward(q):
        here = pair_span(q)
        for c in (2 * q, 2 * q + 1):
            tok_wait(1, c)
            tok_wait(5, c)

        @pl.when(inner == 0)
        def _():
            tok_wait(4, 2 * q)
            tok_wait(4, 2 * q + 1)

        first = 4 * (1 - inner)
        second = 2 + inner
        for n in range(2):
            v = nn(tok[here, half(n)], w[n, 0]) + nn(tok[here, half(1 - n)], w[n, 1])
            v = v + nn(recv[first, here, half(n)], w[n, 2]) + nn(recv[second, here, half(n)], w[n, 3])
            v = v + nn(recv[1, here, half(n)], w[n, 4]) + nn(recv[5, here, half(n)], w[n, 5])
            square = v * v
            t = jnp.tanh(SLOPE * (v + CUBE * (square * v)))
            outv[here, half(n)] = (0.5 * v * (1.0 + t)).astype(BF16)
            slope = 0.5 * (1.0 + t) + 0.5 * v * (1.0 - t * t) * (SLOPE * (1.0 + 3.0 * CUBE * square))
            delta[here, half(n)] = (cot[here, half(n)].astype(F32) * slope).astype(BF16)

    def backward(q):
        here = pair_span(q)
        for b in (0, 3, 2, 1):
            for n in range(2):
                pool[b, here, half(n)] = nt(delta[here, half(n)], w[n, b + 2]).astype(BF16)
            if b == 0:
                @pl.when(inner == 0)
                def _():
                    term_copy(4, 2 * q).start()
                    term_copy(4, 2 * q + 1).start()
            if b == 3:
                term_copy(5, 2 * q).start()
                term_copy(5, 2 * q + 1).start()
        for n in range(2):
            mid = nt(delta[here, half(n)], w[n, 0]).astype(BF16).astype(F32)
            side = nt(delta[here, half(1 - n)], w[1 - n, 1]).astype(BF16).astype(F32)
            acc[here, half(n)] = mid + side

    own(0)

    @pl.loop(0, CHUNKS + LAG)
    def _(i):
        own(i + 1)
        relay(0, 1, i - HOP * (3 - 2 * inner))
        relay(2, 2, i - HOP * (2 - inner))
        relay(3, 3, i - HOP * (3 - inner))
        q = i - LAG

        @pl.when(q == 0)
        def _():
            load_w.wait()
            load_cot.wait()

        @pl.when((q >= 0) & (q % 2 == 0))
        def _():
            forward(q // 2)

        @pl.when((q >= 0) & (q % 2 == 1))
        def _():
            backward(q // 2)

        back_step(q - 1 - BACK)

    def core_copy(k):
        return pltpu.make_async_remote_copy(
            src_ref=other.at[k], dst_ref=crecv.at[k],
            send_sem=c_ssem.at[k], recv_sem=c_rsem.at[k],
            device_id=core_mate, device_id_type=MESH,
        )

    def rs_copy(k, j):
        return pltpu.make_async_remote_copy(
            src_ref=total.at[k, chip_of(j)], dst_ref=rsrecv.at[j - 1, k],
            send_sem=rs_ssem.at[j - 1, k], recv_sem=rs_rsem.at[j - 1, k],
            device_id=mate(j), device_id_type=MESH,
        )

    first = 4 * (1 - inner)
    second = 2 + inner

    def weight_grad(k):
        for n in range(2):
            if k == 0:
                left = tok[:, half(n)]
            elif k == 1:
                left = tok[:, half(1 - n)]
            else:
                left = recv[(first, second, 1, 5)[k - 2], :, half(n)]
            grad = tn(left, delta[:, half(n)])
            grad = grad.reshape(CHIPS, 2, BLK // 16, BLK)
            even, odd = grad[:, 0], grad[:, 1]
            mine[k, :, n] = jnp.where(core == 0, even, odd)
            other[k, :, n] = jnp.where(core == 0, odd, even).astype(BF16)
        core_copy(k).start()

    def pair_sum(k):
        core_copy(k).wait_recv()
        for q in range(CHIPS):
            total[k, q] = (mine[k, q] + crecv[k, q].astype(F32)).astype(BF16)
        for j in range(1, CHIPS):
            rs_copy(k, j).start()

    todo = [(weight_grad, 0), (weight_grad, 1), (weight_grad, 2)]
    for k in range(PARTNERS):
        todo.append((pair_sum, k))
        if k + 3 < PARTNERS:
            todo.append((weight_grad, k + 3))
    for t in range(BACK + 1 + 3 * HOP):
        back_step(CHUNKS - 1 - BACK + t)
        for work, k in todo[t * len(todo) // SPREAD : (t + 1) * len(todo) // SPREAD]:
            work(k)

    def gather_terms(c):
        here = span(c)
        term_wait(4, c)
        term_wait(9, c)

        @pl.when(inner == 1)
        def _():
            term_wait(8, c)
            acc[here, :] += pool[8, here].astype(F32)

        result = acc[here, :] + pool[4, here].astype(F32) + pool[9, here].astype(F32)
        ig[here, :] = result.astype(BF16)

    pl.loop(0, CHUNKS - LAST)(gather_terms)

    @pl.loop(0, PARTNERS)
    def _(k):
        for j in range(1, CHIPS):
            rs_copy(k, j).wait_recv()
        summed = mine[k, chip] + crecv[k, chip].astype(F32)
        for j in range(1, CHIPS):
            summed = summed + rsrecv[j - 1, k].astype(F32)
        for n in range(2):
            wgv[n, k] = summed[n]

    pl.loop(CHUNKS - LAST, CHUNKS)(gather_terms)

    @pl.loop(0, CHUNKS)
    def _(c):
        for flow in (0, 1, 2, 3, 5):
            tok_copy(flow, c).wait_send()
            term_copy(flow, c).wait_send()

        @pl.when(inner == 1)
        def _():
            tok_copy(4, c).wait_send()

        @pl.when(inner == 0)
        def _():
            term_copy(4, c).wait_send()

    @pl.loop(0, PARTNERS)
    def _(k):
        core_copy(k).wait_send()
        for j in range(1, CHIPS):
            rs_copy(k, j).wait_send()


def place(*refs):
    arrays, outs, sem = refs[:3], refs[3:6], refs[6]
    writes = [pltpu.make_async_copy(a, o, sem.at[i]) for i, (a, o) in enumerate(zip(arrays, outs))]
    for write in writes:
        write.start()
    for write in writes:
        write.wait()


def local(tokens, weight, cotangent):
    r, width = tokens.shape
    strip = BLK // 16
    dma = pltpu.SemaphoreType.DMA
    results = pl.pallas_call(
        kernel,
        out_shape=(
            pltpu.VMEM((r, width), BF16),
            pltpu.VMEM((r, width), BF16),
            pltpu.VMEM((2, PARTNERS, strip, BLK), F32),
        ),
        in_specs=[pl.BlockSpec(memory_space=pltpu.HBM)] * 3,
        out_specs=[pl.BlockSpec(memory_space=pltpu.VMEM)] * 3,
        scratch_shapes=[
            pltpu.VMEM((r, width), BF16),
            pltpu.VMEM(weight.shape, BF16),
            pltpu.VMEM((r, width), BF16),
            pltpu.VMEM((FLOWS, r, width), BF16),
            pltpu.VMEM((r, width), BF16),
            pltpu.VMEM((r, width), F32),
            pltpu.VMEM((4 + FLOWS, r, width), BF16),
            pltpu.VMEM((PARTNERS, CHIPS, 2, strip, BLK), F32),
            pltpu.VMEM((PARTNERS, CHIPS, 2, strip, BLK), BF16),
            pltpu.VMEM((PARTNERS, CHIPS, 2, strip, BLK), BF16),
            pltpu.VMEM((PARTNERS, CHIPS, 2, strip, BLK), BF16),
            pltpu.VMEM((CHIPS - 1, PARTNERS, 2, strip, BLK), BF16),
            dma((3,)),
            dma((FLOWS, CHUNKS)),
            dma((FLOWS, CHUNKS)),
            dma((FLOWS, CHUNKS)),
            dma((FLOWS, CHUNKS)),
            dma((PARTNERS,)),
            dma((PARTNERS,)),
            dma((CHIPS - 1, PARTNERS)),
            dma((CHIPS - 1, PARTNERS)),
        ],
        compiler_params=pltpu.CompilerParams(
            collective_id=0, has_side_effects=True, vmem_limit_bytes=63_500_000
        ),
    )(tokens, weight, cotangent)
    return pl.pallas_call(
        place,
        out_shape=tuple(jax.ShapeDtypeStruct(a.shape, a.dtype) for a in results),
        in_specs=[pl.BlockSpec(memory_space=pl.ANY)] * 3,
        out_specs=[pl.BlockSpec(memory_space=pl.ANY)] * 3,
        scratch_shapes=[dma((3,))],
        compiler_params=pltpu.CompilerParams(vmem_limit_bytes=4_000_000),
    )(*results)


def solution(mesh):
    return jax.shard_map(
        local,
        mesh=mesh,
        in_specs=(P("dp", "feat"), P("feat", None, None, None), P("dp", "feat")),
        out_specs=(P("dp", "feat"), P("dp", "feat"), P("feat", None, "dp", None)),
        check_vma=False,
    )
```

```python
import functools

import jax
import jax.numpy as jnp
from jax import lax
from jax.experimental import pallas as pl
from jax.experimental.pallas import tpu as pltpu
from jax.sharding import PartitionSpec as P

F32 = jnp.float32
BF16 = jnp.bfloat16
MESH = pl.DeviceIdType.MESH
BLK = 512
PARTNERS = 6
CHUNKS = 16
HOP = 2
LAG = 9
LAST = 4
SPREAD = 5
EARLY = 6
BACK = 9
FLOWS = 6
CHIPS = 8
SLOPE = 0.7978845608028654
CUBE = 0.044715


def flip(value, bit):
    return value + bit - 2 * bit * ((value // bit) % 2)


def nn(a, b):
    return lax.dot_general(a, b, (((1,), (0,)), ((), ())), preferred_element_type=F32)


def nt(a, b):
    return lax.dot_general(a, b, (((1,), (1,)), ((), ())), preferred_element_type=F32)


def tn(a, b):
    return lax.dot_general(a, b, (((0,), (0,)), ((), ())), preferred_element_type=F32)


def kernel(
    tok_hbm, w_hbm, cot_hbm, outv, ig, wgv,
    tok, w, cot, recv, delta, acc, pool, mine, other, crecv, total, rsrecv,
    load_sem, tok_ssem, tok_rsem, term_ssem, term_rsem, c_ssem, c_rsem, rs_ssem, rs_rsem,
):
    rows = tok.shape[0] // CHUNKS
    d = lax.axis_index("dp")
    f = lax.axis_index("feat")
    core = d % 2
    chip = d // 2
    y = chip // 2
    x_lo = chip % 2
    z = f % 8
    inner = (z + z // 2) % 2
    sgn = 1 - 2 * ((z // 2) % 2)

    def along(step):
        return (d, (f // 8) * 8 + (z + step + 8) % 8)

    ahead = along(sgn)
    behind = along(-sgn)
    across = (d, flip(f, 8))
    core_mate = (flip(d, 1), f)

    def chip_of(j):
        dy, dx = j // 2, j % 2
        return ((y + dy) % 4) * 2 + (x_lo + dx) % 2

    def mate(j):
        return (chip_of(j) * 2 + core, f)

    everyone = [ahead, behind, across, core_mate]
    barrier = pltpu.get_barrier_semaphore()
    for who in everyone:
        pl.semaphore_signal(barrier, inc=1, device_id=who, device_id_type=MESH)
    for j in range(1, CHIPS):
        pl.semaphore_signal(barrier, inc=1, device_id=mate(j), device_id_type=MESH)

    load_tok = pltpu.make_async_copy(tok_hbm, tok, load_sem.at[0])
    load_w = pltpu.make_async_copy(w_hbm, w, load_sem.at[1])
    load_cot = pltpu.make_async_copy(cot_hbm, cot, load_sem.at[2])
    load_tok.start()
    load_w.start()
    load_cot.start()
    pl.semaphore_wait(barrier, len(everyone) + CHIPS - 1)
    load_tok.wait()

    def span(c):
        return pl.ds(pl.multiple_of(c * rows, rows), rows)

    def pair_span(q):
        return pl.ds(pl.multiple_of(q * 2 * rows, 2 * rows), 2 * rows)

    def half(n):
        return pl.ds(n * BLK, BLK)

    def tok_copy(flow, c):
        source, slot, to = (
            (tok.at[span(c)], 2 * inner, ahead),
            (recv.at[0, span(c)], 2 * inner + 1, ahead),
            (recv.at[2, span(c)], 2 * inner, behind),
            (recv.at[3, span(c)], 2 * inner + 1, behind),
            (tok.at[span(c)], 4, behind),
            (tok.at[span(c)], 5, across),
        )[flow]
        return pltpu.make_async_remote_copy(
            src_ref=source, dst_ref=recv.at[slot, span(c)],
            send_sem=tok_ssem.at[flow, c], recv_sem=tok_rsem.at[slot, c],
            device_id=to, device_id_type=MESH,
        )

    def tok_wait(slot, c):
        pltpu.make_async_remote_copy(
            src_ref=recv.at[slot, span(c)], dst_ref=recv.at[slot, span(c)],
            send_sem=tok_ssem.at[0, c], recv_sem=tok_rsem.at[slot, c],
            device_id=ahead, device_id_type=MESH,
        ).wait_recv()

    def own(c):
        @pl.when(c < CHUNKS)
        def _():
            tok_copy(0, c).start()
            tok_copy(5, c).start()

            @pl.when(inner == 1)
            def _():
                tok_copy(4, c).start()

    def relay(slot, flow, c):
        @pl.when((c >= 0) & (c < CHUNKS))
        def _():
            tok_wait(slot, c)
            tok_copy(flow, c).start()

    low = 4 + 2 * (1 - inner)

    def term_copy(flow, c):
        source, slot, to = (
            (5 * (1 - inner), low, behind),
            (2, low + 1, behind),
            (1 + 5 * inner, low, ahead),
            (1 + 6 * (1 - inner), low + 1, ahead),
            (0, 8, ahead),
            (3, 9, across),
        )[flow]
        return pltpu.make_async_remote_copy(
            src_ref=pool.at[source, span(c)], dst_ref=pool.at[slot, span(c)],
            send_sem=term_ssem.at[flow, c], recv_sem=term_rsem.at[slot - 4, c],
            device_id=to, device_id_type=MESH,
        )

    def term_wait(slot, c):
        pltpu.make_async_remote_copy(
            src_ref=pool.at[slot, span(c)], dst_ref=pool.at[slot, span(c)],
            send_sem=term_ssem.at[0, c], recv_sem=term_rsem.at[slot - 4, c],
            device_id=ahead, device_id_type=MESH,
        ).wait_recv()

    def add_term(into, slot, c):
        here = span(c)
        pool[into, here] = (pool[into, here].astype(F32) + pool[slot, here].astype(F32)).astype(BF16)

    def back_step(p):
        c1 = p + EARLY * (1 - inner)

        @pl.when((c1 >= 0) & (c1 < CHUNKS))
        def _():
            term_copy(1, c1).start()

        c0 = p - HOP * (1 + 2 * inner) + EARLY * inner

        @pl.when((c0 >= 0) & (c0 < CHUNKS))
        def _():
            term_wait(5, c0)

            @pl.when(inner == 1)
            def _():
                add_term(0, 5, c0)

            term_copy(0, c0).start()

        c2 = p - HOP * (2 + inner)

        @pl.when((c2 >= 0) & (c2 < CHUNKS))
        def _():
            term_wait(6, c2)

            @pl.when(inner == 0)
            def _():
                add_term(1, 6, c2)

            term_copy(2, c2).start()

        c3 = p - HOP * (1 + inner) + EARLY

        @pl.when((c3 >= 0) & (c3 < CHUNKS))
        def _():
            term_wait(7, c3)

            @pl.when(inner == 1)
            def _():
                add_term(1, 7, c3)

            term_copy(3, c3).start()

    def forward(q):
        here = pair_span(q)
        for c in (2 * q, 2 * q + 1):
            tok_wait(1, c)
            tok_wait(5, c)

        @pl.when(inner == 0)
        def _():
            tok_wait(4, 2 * q)
            tok_wait(4, 2 * q + 1)

        first = 4 * (1 - inner)
        second = 2 + inner
        for n in range(2):
            v = nn(tok[here, half(n)], w[n, 0]) + nn(tok[here, half(1 - n)], w[n, 1])
            v = v + nn(recv[first, here, half(n)], w[n, 2]) + nn(recv[second, here, half(n)], w[n, 3])
            v = v + nn(recv[1, here, half(n)], w[n, 4]) + nn(recv[5, here, half(n)], w[n, 5])
            square = v * v
            t = jnp.tanh(SLOPE * (v + CUBE * (square * v)))
            outv[here, half(n)] = (0.5 * v * (1.0 + t)).astype(BF16)
            slope = 0.5 * (1.0 + t) + 0.5 * v * (1.0 - t * t) * (SLOPE * (1.0 + 3.0 * CUBE * square))
            delta[here, half(n)] = (cot[here, half(n)].astype(F32) * slope).astype(BF16)

    def backward(q):
        here = pair_span(q)
        for b in (0, 3, 2, 1):
            for n in range(2):
                pool[b, here, half(n)] = nt(delta[here, half(n)], w[n, b + 2]).astype(BF16)
            if b == 0:
                @pl.when(inner == 0)
                def _():
                    term_copy(4, 2 * q).start()
                    term_copy(4, 2 * q + 1).start()
            if b == 3:
                term_copy(5, 2 * q).start()
                term_copy(5, 2 * q + 1).start()
        for n in range(2):
            mid = nt(delta[here, half(n)], w[n, 0]).astype(BF16).astype(F32)
            side = nt(delta[here, half(1 - n)], w[1 - n, 1]).astype(BF16).astype(F32)
            acc[here, half(n)] = mid + side

    own(0)

    @pl.loop(0, CHUNKS + LAG)
    def _(i):
        own(i + 1)
        relay(0, 1, i - HOP * (3 - 2 * inner))
        relay(2, 2, i - HOP * (2 - inner))
        relay(3, 3, i - HOP * (3 - inner))
        q = i - LAG

        @pl.when(q == 0)
        def _():
            load_w.wait()
            load_cot.wait()

        @pl.when((q >= 0) & (q % 2 == 0))
        def _():
            forward(q // 2)

        @pl.when((q >= 0) & (q % 2 == 1))
        def _():
            backward(q // 2)

        back_step(q - 1 - BACK)

    def core_copy(k):
        return pltpu.make_async_remote_copy(
            src_ref=other.at[k], dst_ref=crecv.at[k],
            send_sem=c_ssem.at[k], recv_sem=c_rsem.at[k],
            device_id=core_mate, device_id_type=MESH,
        )

    def rs_copy(k, j):
        return pltpu.make_async_remote_copy(
            src_ref=total.at[k, chip_of(j)], dst_ref=rsrecv.at[j - 1, k],
            send_sem=rs_ssem.at[j - 1, k], recv_sem=rs_rsem.at[j - 1, k],
            device_id=mate(j), device_id_type=MESH,
        )

    first = 4 * (1 - inner)
    second = 2 + inner

    def weight_grad(k):
        for n in range(2):
            if k == 0:
                left = tok[:, half(n)]
            elif k == 1:
                left = tok[:, half(1 - n)]
            else:
                left = recv[(first, second, 1, 5)[k - 2], :, half(n)]
            grad = tn(left, delta[:, half(n)])
            grad = grad.reshape(CHIPS, 2, BLK // 16, BLK)
            even, odd = grad[:, 0], grad[:, 1]
            mine[k, :, n] = jnp.where(core == 0, even, odd)
            other[k, :, n] = jnp.where(core == 0, odd, even).astype(BF16)
        core_copy(k).start()

    def pair_sum(k):
        core_copy(k).wait_recv()
        for q in range(CHIPS):
            total[k, q] = (mine[k, q] + crecv[k, q].astype(F32)).astype(BF16)
        for j in range(1, CHIPS):
            rs_copy(k, j).start()

    todo = [(weight_grad, 0), (weight_grad, 1), (weight_grad, 2)]
    for k in range(PARTNERS):
        todo.append((pair_sum, k))
        if k + 3 < PARTNERS:
            todo.append((weight_grad, k + 3))
    for t in range(BACK + 1 + 3 * HOP):
        back_step(CHUNKS - 1 - BACK + t)
        for work, k in todo[t * len(todo) // SPREAD : (t + 1) * len(todo) // SPREAD]:
            work(k)

    def gather_terms(c):
        here = span(c)
        term_wait(4, c)
        term_wait(9, c)

        @pl.when(inner == 1)
        def _():
            term_wait(8, c)
            acc[here, :] += pool[8, here].astype(F32)

        result = acc[here, :] + pool[4, here].astype(F32) + pool[9, here].astype(F32)
        ig[here, :] = result.astype(BF16)

    pl.loop(0, CHUNKS - LAST)(gather_terms)

    @pl.loop(0, PARTNERS)
    def _(k):
        for j in range(1, CHIPS):
            rs_copy(k, j).wait_recv()
        summed = mine[k, chip] + crecv[k, chip].astype(F32)
        for j in range(1, CHIPS):
            summed = summed + rsrecv[j - 1, k].astype(F32)
        for n in range(2):
            wgv[n, k] = summed[n]

    pl.loop(CHUNKS - LAST, CHUNKS)(gather_terms)

    @pl.loop(0, CHUNKS)
    def _(c):
        for flow in (0, 1, 2, 3, 5):
            tok_copy(flow, c).wait_send()
            term_copy(flow, c).wait_send()

        @pl.when(inner == 1)
        def _():
            tok_copy(4, c).wait_send()

        @pl.when(inner == 0)
        def _():
            term_copy(4, c).wait_send()

    @pl.loop(0, PARTNERS)
    def _(k):
        core_copy(k).wait_send()
        for j in range(1, CHIPS):
            rs_copy(k, j).wait_send()


def place(*refs):
    arrays, outs, sem = refs[:3], refs[3:6], refs[6]
    writes = [pltpu.make_async_copy(a, o, sem.at[i]) for i, (a, o) in enumerate(zip(arrays, outs))]
    for write in writes:
        write.start()
    for write in writes:
        write.wait()


def local(tokens, weight, cotangent):
    r, width = tokens.shape
    strip = BLK // 16
    dma = pltpu.SemaphoreType.DMA
    results = pl.pallas_call(
        kernel,
        out_shape=(
            pltpu.VMEM((r, width), BF16),
            pltpu.VMEM((r, width), BF16),
            pltpu.VMEM((2, PARTNERS, strip, BLK), F32),
        ),
        in_specs=[pl.BlockSpec(memory_space=pltpu.HBM)] * 3,
        out_specs=[pl.BlockSpec(memory_space=pltpu.VMEM)] * 3,
        scratch_shapes=[
            pltpu.VMEM((r, width), BF16),
            pltpu.VMEM(weight.shape, BF16),
            pltpu.VMEM((r, width), BF16),
            pltpu.VMEM((FLOWS, r, width), BF16),
            pltpu.VMEM((r, width), BF16),
            pltpu.VMEM((r, width), F32),
            pltpu.VMEM((4 + FLOWS, r, width), BF16),
            pltpu.VMEM((PARTNERS, CHIPS, 2, strip, BLK), F32),
            pltpu.VMEM((PARTNERS, CHIPS, 2, strip, BLK), BF16),
            pltpu.VMEM((PARTNERS, CHIPS, 2, strip, BLK), BF16),
            pltpu.VMEM((PARTNERS, CHIPS, 2, strip, BLK), BF16),
            pltpu.VMEM((CHIPS - 1, PARTNERS, 2, strip, BLK), BF16),
            dma((3,)),
            dma((FLOWS, CHUNKS)),
            dma((FLOWS, CHUNKS)),
            dma((FLOWS, CHUNKS)),
            dma((FLOWS, CHUNKS)),
            dma((PARTNERS,)),
            dma((PARTNERS,)),
            dma((CHIPS - 1, PARTNERS)),
            dma((CHIPS - 1, PARTNERS)),
        ],
        compiler_params=pltpu.CompilerParams(
            collective_id=0, has_side_effects=True, vmem_limit_bytes=63_500_000
        ),
    )(tokens, weight, cotangent)
    return pl.pallas_call(
        place,
        out_shape=tuple(jax.ShapeDtypeStruct(a.shape, a.dtype) for a in results),
        in_specs=[pl.BlockSpec(memory_space=pl.ANY)] * 3,
        out_specs=[pl.BlockSpec(memory_space=pl.ANY)] * 3,
        scratch_shapes=[dma((3,))],
        compiler_params=pltpu.CompilerParams(vmem_limit_bytes=4_000_000),
    )(*results)


def solution(mesh):
    return jax.shard_map(
        local,
        mesh=mesh,
        in_specs=(P("dp", "feat"), P("feat", None, None, None), P("dp", "feat")),
        out_specs=(P("dp", "feat"), P("dp", "feat"), P("feat", None, "dp", None)),
        check_vma=False,
    )
```
